512 devices in a mesh: ctx: 512 (over x, z, y, core).
Axes of the slice: x: 4, y: 4, z: 16, core: 2. Of those that a mesh axis runs over, the one named last changes fastest.
Arguments:
- queries: bfloat16 [65536, 16, 128], P('ctx'), may hold values from -6 to 6
- keys: bfloat16 [65536, 8, 128], P('ctx'), may hold values from -5 to 5
- values: bfloat16 [65536, 8, 128], P('ctx'), may hold values from -6 to 6
- d_out: bfloat16 [65536, 16, 128], P('ctx'), may hold values from -48 to 48
Outputs:
- grad_queries: bfloat16 [65536, 16, 128], P('ctx')
- grad_keys: bfloat16 [65536, 8, 128], P('ctx')
- grad_values: bfloat16 [65536, 8, 128], P('ctx')
The draws below stay inside these ranges and needn't reach their ends.
All inputs are finite; a program needn't handle non-finite values.
Results may differ from the reference program's by a relative error of at most 0.012.
The reference program's roundings to bfloat16 on the way count: a program that leaves them out, or rounds other values in their place, can miss the bound.
Values may be sent and summed in bfloat16 or wider, within the bound.
A program may use at most 64 MiB of HBM per device.

```python
import jax
import jax.numpy as jnp
from jax import lax

HEADS = 16
KV_HEADS = 8
HEAD_WIDTH = 128
WINDOW = 512
TOK_DEV = 128
TOKENS = 65536


def draw_queries(key, part):
    result = jax.random.normal(jax.random.fold_in(key, 11), (TOKENS, HEADS, HEAD_WIDTH), jnp.float32)
    result = jnp.clip(result, -5.0, 5.0)
    return result.astype(jnp.bfloat16)


def draw_keys(key, part):
    result = jax.random.normal(jax.random.fold_in(key, 13), (TOKENS, KV_HEADS, HEAD_WIDTH), jnp.float32)
    result = jnp.clip(result, -5.0, 5.0)
    return result.astype(jnp.bfloat16)


def shard_levels(stream_key, shape, shards, low, largest):
    loudness = 1.0
    for dim, parts in shards:
        heights = jax.random.uniform(jax.random.fold_in(jax.random.fold_in(stream_key, 6), dim), (parts,), jnp.float32, low / len(shards), largest / len(shards))
        loudness = loudness * jnp.repeat(jnp.exp(heights), shape[dim] // parts).reshape((-1,) + (1,) * (len(shape) - 1 - dim))
    return loudness


def gaussian(rng, dims, spread, bound, split=(), kind=jnp.bfloat16):
    drawn = spread * jax.random.normal(rng, dims, jnp.float32)
    if split:
        drawn = drawn * shard_levels(rng, dims, split, -0.22, 0.18)
    return jnp.clip(drawn, -bound, bound).astype(kind)


def setup_inputs(seed: int = 0) -> dict:
    key_of = jax.random.split(jax.random.key(seed), 5)
    queries = draw_queries(jax.random.fold_in(key_of[4], 71), 0)
    keys = draw_keys(jax.random.fold_in(key_of[4], 71), 0)
    values = gaussian(key_of[2], (TOKENS, KV_HEADS, HEAD_WIDTH), 1.0, 6.0, ((0, 512),))
    d_out = gaussian(key_of[3], (TOKENS, HEADS, HEAD_WIDTH), 8.0, 48.0, ((0, 512),))
    return dict(queries=queries, keys=keys, values=values, d_out=d_out)


score_scale = 168.0 ** -0.5


def block_grads(queries_blk, keys_win, values_win, block_gradient, row_start):
    row_count = queries_blk.shape[0]
    key_span = keys_win.shape[0]
    group_size = HEADS // KV_HEADS
    grouped = queries_blk.reshape(row_count, KV_HEADS, group_size, HEAD_WIDTH).astype(jnp.float32)
    gradient_per_group = block_gradient.reshape(row_count, KV_HEADS, group_size, HEAD_WIDTH).astype(jnp.float32)
    keys_wide = keys_win.astype(jnp.float32)
    widened_values = values_win.astype(jnp.float32)
    scores = jnp.einsum("tgre,jge->grtj", grouped, keys_wide) * score_scale
    query_pos = row_start + jnp.arange(row_count, dtype=jnp.int32)
    key_pos = row_start - WINDOW + jnp.arange(key_span, dtype=jnp.int32)
    distance = query_pos[:, None] - key_pos[None, :]
    visible = (distance >= 0) & (distance < WINDOW) & (key_pos[None, :] >= 0)
    scores = jnp.where(visible, scores, -jnp.inf)
    row_max = jnp.max(scores, axis=-1, keepdims=True)
    row_sum = jnp.sum(jnp.exp(scores - row_max), axis=-1, keepdims=True)
    log_total = row_max + jnp.log(row_sum)
    probability = jnp.exp(scores - log_total)
    probs_low = lax.optimization_barrier(probability.astype(jnp.bfloat16))
    attention_result_rows = jnp.einsum("grtj,jge->tgre", probs_low.astype(jnp.float32), widened_values).astype(jnp.bfloat16)
    attention_result_rows = lax.optimization_barrier(attention_result_rows)
    row_dot_product = jnp.einsum("vwhn,vwhn->whv", gradient_per_group, attention_result_rows.astype(jnp.float32))
    grad_probs = jnp.einsum("tgre,jge->grtj", gradient_per_group, widened_values)
    grad_scores = lax.optimization_barrier((probability * (grad_probs - row_dot_product[..., None])).astype(jnp.bfloat16))
    grad_scores_wide = grad_scores.astype(jnp.float32)
    query_gradient = (jnp.einsum("grtj,jge->tgre", grad_scores_wide, keys_wide) * score_scale).astype(jnp.bfloat16)
    grad_key = jnp.einsum("grtj,tgre->jge", grad_scores_wide, grouped) * score_scale
    grad_value = jnp.einsum("grtj,tgre->jge", probs_low.astype(jnp.float32), gradient_per_group)
    return query_gradient.reshape(row_count, HEADS, HEAD_WIDTH), grad_key, grad_value


def reference(queries, keys, values, d_out):
    blocks = TOKENS // TOK_DEV
    key_span = WINDOW + TOK_DEV
    front_pad = jnp.zeros((WINDOW, KV_HEADS, HEAD_WIDTH), keys.dtype)
    padded_keys = jnp.concatenate([front_pad, keys], axis=0)
    values_pad = jnp.concatenate([front_pad, values], axis=0)

    def advance(running, block_index):
        row_start = (block_index * TOK_DEV).astype(jnp.int32)
        queries_blk = lax.dynamic_slice_in_dim(queries, row_start, TOK_DEV, 0)
        block_gradient = lax.dynamic_slice_in_dim(d_out, row_start, TOK_DEV, 0)
        keys_win = lax.dynamic_slice_in_dim(padded_keys, row_start, key_span, 0)
        values_win = lax.dynamic_slice_in_dim(values_pad, row_start, key_span, 0)
        query_gradient, grad_key, grad_value = block_grads(queries_blk, keys_win, values_win, block_gradient, row_start)
        key_acc, value_acc = running
        key_acc = lax.dynamic_update_slice_in_dim(key_acc, lax.dynamic_slice_in_dim(key_acc, row_start, key_span, 0) + grad_key, row_start, 0)
        value_acc = lax.dynamic_update_slice_in_dim(value_acc, lax.dynamic_slice_in_dim(value_acc, row_start, key_span, 0) + grad_value, row_start, 0)
        return (key_acc, value_acc), query_gradient

    empty_totals = jnp.zeros((TOKENS + WINDOW, KV_HEADS, HEAD_WIDTH), jnp.float32)
    (key_acc, value_acc), grad_blocks = lax.scan(advance, (empty_totals, empty_totals), jnp.arange(blocks, dtype=jnp.int32))
    grad_queries = grad_blocks.reshape(TOKENS, HEADS, HEAD_WIDTH)
    return grad_queries, key_acc[WINDOW:].astype(jnp.bfloat16), value_acc[WINDOW:].astype(jnp.bfloat16)
```

```python
import functools

import jax
import jax.numpy as jnp
from jax import lax
from jax.experimental import pallas as pl
from jax.experimental.pallas import tpu as pltpu
from jax.sharding import PartitionSpec as P

HEADS = 16
KV_HEADS = 8
HEAD_WIDTH = 128
WINDOW = 512
TOK_DEV = 128
GROUP = HEADS // KV_HEADS
CHIP_TOK = 2 * TOK_DEV
SPAN = WINDOW + CHIP_TOK
REACH = WINDOW + TOK_DEV
ROWS = GROUP * TOK_DEV
MINE = KV_HEADS // 2

MESH = pl.DeviceIdType.MESH
SCALE = 168.0 ** (-0.5)
F32 = jnp.float32
BF16 = jnp.bfloat16


def dot(a, b, contract):
    return lax.dot_general(a, b, ((contract[:1], contract[1:]), ((), ())), preferred_element_type=F32)


def kernel(
    n, kv_in, qd_in, dq_out, dkv_out,
    kvb, qdb, acc, p0_out, p0_in, s_out, s_in, dq_send, dkv_send,
    loc_kv, loc_qd, xkv_s, xkv_r, xqd_s, xqd_r, own_s, own_r, fwd_s, fwd_r,
    p0_s, p0_r, sum_s, sum_r, dq_s, dq_r, dkv_s, dkv_r,
):
    me = lax.axis_index("ctx")
    chip = me // 2
    core = me % 2
    other = 1 - core
    partner = chip * 2 + other
    ahead = (me + 2) % n
    ahead_other = (partner + 2) % n
    behind = (me + n - 2) % n
    behind_other = (partner + n - 2) % n

    barrier = pltpu.get_barrier_semaphore()
    for peer in (partner, ahead, ahead_other, behind, behind_other):
        pl.semaphore_signal(barrier, inc=1, device_id=(peer,), device_id_type=MESH)
    pl.semaphore_wait(barrier, 5)

    def remote(src, dst, send, recv, target):
        return pltpu.make_async_remote_copy(
            src_ref=src, dst_ref=dst, send_sem=send, recv_sem=recv, device_id=(target,), device_id_type=MESH
        )

    my_tok = pl.ds(pl.multiple_of(core * TOK_DEV, TOK_DEV), TOK_DEV)
    my_key = pl.ds(pl.multiple_of(WINDOW + core * TOK_DEV, TOK_DEV), TOK_DEV)
    my_back = pl.ds(pl.multiple_of(CHIP_TOK + core * TOK_DEV, TOK_DEV), TOK_DEV)
    my_row = pl.ds(pl.multiple_of(core * ROWS, ROWS), ROWS)
    other_tok = pl.ds(pl.multiple_of(WINDOW + other * TOK_DEV, TOK_DEV), TOK_DEV)
    other_row = pl.ds(pl.multiple_of(other * ROWS, ROWS), ROWS)

    def local_kv(h):
        return pltpu.make_async_copy(kv_in.at[core * MINE + h], kvb.at[h, :, my_key, :], loc_kv.at[h])

    def local_qd(h):
        return pltpu.make_async_copy(qd_in.at[core * MINE + h], qdb.at[h, :, my_row, :], loc_qd.at[h])

    def swap_kv(h):
        return remote(kv_in.at[other * MINE + h], kvb.at[h, :, my_key, :], xkv_s.at[h], xkv_r.at[h], partner)

    def swap_qd(h):
        return remote(qd_in.at[other * MINE + h], qdb.at[h, :, my_row, :], xqd_s.at[h], xqd_r.at[h], partner)

    def own_same(h):
        return remote(kv_in.at[core * MINE + h], kvb.at[h, :, my_back, :], own_s.at[h, 0], own_r.at[h, core], ahead)

    def own_cross(h):
        return remote(kv_in.at[other * MINE + h], kvb.at[h, :, my_back, :], own_s.at[h, 1], own_r.at[h, core], ahead_other)

    def came(h, j):
        tok = pl.ds(CHIP_TOK + j * TOK_DEV, TOK_DEV)
        return remote(kvb.at[h, :, tok, :], kvb.at[h, :, tok, :], own_s.at[h, j], own_r.at[h, j], ahead)

    def relay(h):
        return remote(
            kvb.at[h, :, pl.ds(CHIP_TOK, CHIP_TOK), :], kvb.at[h, :, pl.ds(0, CHIP_TOK), :], fwd_s.at[h], fwd_r.at[h], ahead
        )

    def far(h):
        return remote(p0_out.at[h], p0_in.at[h], p0_s.at[h], p0_r.at[h], behind)

    def near(h):
        return remote(s_out.at[h], s_in.at[h], sum_s.at[h], sum_r.at[h], behind)

    def give_dq(h):
        return remote(dq_send.at[h], dq_out.at[core * MINE + h], dq_s.at[h], dq_r.at[h], partner)

    def take_dq(h):
        return remote(dq_send.at[h], dq_out.at[other * MINE + h], dq_s.at[h], dq_r.at[h], partner)

    def give_dkv(h):
        return remote(dkv_send.at[h], dkv_out.at[core * MINE + h], dkv_s.at[h], dkv_r.at[h], partner)

    def take_dkv(h):
        return remote(dkv_send.at[h], dkv_out.at[other * MINE + h], dkv_s.at[h], dkv_r.at[h], partner)

    def send_own(h):
        own_same(h).start()
        own_cross(h).start()

    def pass_on(h):
        came(h, 0).wait_recv()
        came(h, 1).wait_recv()
        relay(h).start()

    send_own(0)
    for h in range(MINE):
        local_kv(h).start()
        local_qd(h).start()
        swap_kv(h).start()
        swap_qd(h).start()
        if h == 0:
            send_own(1)
    pass_on(0)
    send_own(2)

    first_key = WINDOW - CHIP_TOK * chip

    def half(h, b):
        key_at = pl.ds(b * TOK_DEV, REACH)
        row_at = pl.ds(b * ROWS, ROWS)
        k = kvb[h, 0, key_at, :]
        v = kvb[h, 1, key_at, :]
        q = qdb[h, 0, row_at, :]
        do = qdb[h, 1, row_at, :]
        s = dot(k, q, (1, 1))
        key_pos = lax.broadcasted_iota(jnp.int32, (REACH, ROWS), 0)
        query_pos = lax.broadcasted_iota(jnp.int32, (REACH, ROWS), 1) // GROUP
        distance = key_pos - query_pos
        visible = (distance > 0) & (distance <= WINDOW) & (key_pos >= first_key - b * TOK_DEV)
        s = jnp.where(visible, s, -1e30)
        top = jnp.max(s, axis=0, keepdims=True)
        e = jnp.exp((s - top) * SCALE)
        p = e * (1.0 / jnp.sum(e, axis=0, keepdims=True))
        low = p.astype(BF16)
        o = dot(v, low, (0, 0)).astype(BF16).astype(F32)
        row_dot = jnp.sum(o * do.astype(F32).T, axis=0, keepdims=True)
        gp = dot(v, do, (1, 1))
        gs = (p * (gp - row_dot)).astype(BF16)
        dv = dot(low, do, (1, 0))
        dk = dot(gs, q, (1, 0)) * SCALE
        dq = (dot(k, gs, (0, 0)) * SCALE).T.astype(BF16)
        if b == 0:
            acc[h, 0, pl.ds(0, REACH), :] = dk
            acc[h, 1, pl.ds(0, REACH), :] = dv
            acc[h, 0, pl.ds(REACH, TOK_DEV), :] = jnp.zeros((TOK_DEV, HEAD_WIDTH), F32)
            acc[h, 1, pl.ds(REACH, TOK_DEV), :] = jnp.zeros((TOK_DEV, HEAD_WIDTH), F32)
        else:
            acc[h, 0, key_at, :] += dk
            acc[h, 1, key_at, :] += dv

        @pl.when(core == b)
        def _():
            dq_out[core * MINE + h] = dq

        @pl.when(core != b)
        def _():
            dq_send[h] = dq

    def add_near(h):
        far(h).wait_recv()
        s_out[h] = (acc[h, :, pl.ds(CHIP_TOK, CHIP_TOK), :] + p0_in[h].astype(F32)).astype(BF16)
        near(h).start()

    def finish(h):
        near(h).wait_recv()
        dkv_send[h] = (acc[h, :, other_tok, :] + s_in[h, :, pl.ds(pl.multiple_of(other * TOK_DEV, TOK_DEV), TOK_DEV), :].astype(F32)).astype(BF16)
        give_dkv(h).start()
        dkv_out[core * MINE + h] = (acc[h, :, my_key, :] + s_in[h, :, my_tok, :].astype(F32)).astype(BF16)

    def step(h, carry):
        @pl.when(h + 1 < MINE)
        def _():
            pass_on(h + 1)

        @pl.when(h + 3 < MINE)
        def _():
            send_own(h + 3)

        local_kv(h).wait()
        local_qd(h).wait()
        swap_kv(h).wait_recv()
        swap_qd(h).wait_recv()
        relay(h).wait_recv()
        half(h, 0)
        half(h, 1)
        p0_out[h] = acc[h, :, pl.ds(0, CHIP_TOK), :].astype(BF16)
        far(h).start()
        give_dq(h).start()

        @pl.when(h >= 1)
        def _():
            add_near(h - 1)

        @pl.when(h >= 2)
        def _():
            finish(h - 2)

        return carry

    lax.fori_loop(0, MINE, step, 0)
    finish(MINE - 2)
    add_near(MINE - 1)
    finish(MINE - 1)

    for h in range(MINE):
        take_dq(h).wait_recv()
        take_dkv(h).wait_recv()
        swap_kv(h).wait_send()
        swap_qd(h).wait_send()
        own_same(h).wait_send()
        own_cross(h).wait_send()
        relay(h).wait_send()
        far(h).wait_send()
        near(h).wait_send()
        give_dq(h).wait_send()
        give_dkv(h).wait_send()


def body(n, queries, keys, values, d_out):
    kv = jnp.stack([keys, values]).transpose(2, 0, 1, 3)
    qd = jnp.stack([queries, d_out]).reshape(2, TOK_DEV, KV_HEADS, GROUP, HEAD_WIDTH)
    qd = qd.transpose(2, 0, 1, 3, 4).reshape(KV_HEADS, 2, ROWS, HEAD_WIDTH)
    dma = pltpu.SemaphoreType.DMA
    dq, dkv = pl.pallas_call(
        functools.partial(kernel, n),
        out_shape=(
            jax.ShapeDtypeStruct((KV_HEADS, ROWS, HEAD_WIDTH), BF16),
            jax.ShapeDtypeStruct((KV_HEADS, 2, TOK_DEV, HEAD_WIDTH), BF16),
        ),
        in_specs=[pl.BlockSpec(memory_space=pl.ANY)] * 2,
        out_specs=(pl.BlockSpec(memory_space=pltpu.VMEM), pl.BlockSpec(memory_space=pltpu.VMEM)),
        scratch_shapes=[
            pltpu.VMEM((MINE, 2, SPAN, HEAD_WIDTH), BF16),
            pltpu.VMEM((MINE, 2, 2 * ROWS, HEAD_WIDTH), BF16),
            pltpu.VMEM((MINE, 2, SPAN, HEAD_WIDTH), F32),
            pltpu.VMEM((MINE, 2, CHIP_TOK, HEAD_WIDTH), BF16),
            pltpu.VMEM((MINE, 2, CHIP_TOK, HEAD_WIDTH), BF16),
            pltpu.VMEM((MINE, 2, CHIP_TOK, HEAD_WIDTH), BF16),
            pltpu.VMEM((MINE, 2, CHIP_TOK, HEAD_WIDTH), BF16),
            pltpu.VMEM((MINE, ROWS, HEAD_WIDTH), BF16),
            pltpu.VMEM((MINE, 2, TOK_DEV, HEAD_WIDTH), BF16),
        ]
        + [dma((MINE,))] * 6
        + [dma((MINE, 2))] * 2
        + [dma((MINE,))] * 10,
        compiler_params=pltpu.CompilerParams(collective_id=0, has_side_effects=True, vmem_limit_bytes=48 * 2**20),
    )(kv, qd)
    dq = dq.reshape(KV_HEADS, TOK_DEV, GROUP, HEAD_WIDTH).transpose(1, 0, 2, 3).reshape(TOK_DEV, HEADS, HEAD_WIDTH)
    dkv = dkv.transpose(1, 2, 0, 3)
    return dq, dkv[0], dkv[1]


def solution(mesh):
    placed = P("ctx", None, None)
    return jax.shard_map(
        functools.partial(body, mesh.shape["ctx"]),
        mesh=mesh,
        in_specs=(placed,) * 4,
        out_specs=(placed,) * 3,
        check_vma=False,
    )
```

```python
import functools

import jax
import jax.numpy as jnp
from jax import lax
from jax.experimental import pallas as pl
from jax.experimental.pallas import tpu as pltpu
from jax.sharding import PartitionSpec as P

HEADS = 16
KV_HEADS = 8
HEAD_WIDTH = 128
WINDOW = 512
TOK_DEV = 128
GROUP = HEADS // KV_HEADS
CHIP_TOK = 2 * TOK_DEV
SPAN = WINDOW + CHIP_TOK
REACH = WINDOW + TOK_DEV
ROWS = GROUP * TOK_DEV
MINE = KV_HEADS // 2

MESH = pl.DeviceIdType.MESH
SCALE = 168.0 ** (-0.5)
F32 = jnp.float32
BF16 = jnp.bfloat16


def dot(a, b, contract):
    return lax.dot_general(a, b, ((contract[:1], contract[1:]), ((), ())), preferred_element_type=F32)


def kernel(
    n, q_in, k_in, v_in, do_in, dq_out, dk_out, dv_out,
    kraw, qraw, kwide, qwide, kv_in, qd_in, dq_wide, dkv_wide,
    kvb, qdb, acc, p0_out, p0_in, s_out, s_in, dq_send, dkv_send, dq_got, dkv_got,
    raw_s, loc_kv, loc_qd, xkv_s, xkv_r, xqd_s, xqd_r, own_s, own_r, fwd_s, fwd_r,
    p0_s, p0_r, sum_s, sum_r, dq_s, dq_r, dkv_s, dkv_r,
):
    me = lax.axis_index("ctx")
    chip = me // 2
    core = me % 2
    other = 1 - core
    partner = chip * 2 + other
    ahead = (me + 2) % n
    ahead_other = (partner + 2) % n
    behind = (me + n - 2) % n
    behind_other = (partner + n - 2) % n
    last = n // 2 - 1
    has_ahead = chip < last
    has_behind = chip > 0
    has_far = chip > 1

    barrier = pltpu.get_barrier_semaphore()

    def greet(*peers):
        for peer in peers:
            pl.semaphore_signal(barrier, inc=1, device_id=(peer,), device_id_type=MESH)

    greet(partner)
    pl.when(has_ahead)(lambda: greet(ahead, ahead_other))
    pl.when(has_behind)(lambda: greet(behind, behind_other))

    raws = [
        pltpu.make_async_copy(src, dst, raw_s.at[i])
        for i, (src, dst) in enumerate(
            ((k_in, kraw.at[0]), (v_in, kraw.at[1]), (q_in, qraw.at[0]), (do_in, qraw.at[1]))
        )
    ]
    for copy in raws:
        copy.start()
    for i in (0, 1):
        raws[i].wait()
        kwide[i] = kraw[i].astype(F32).reshape(TOK_DEV * KV_HEADS, HEAD_WIDTH)
    for g in range(KV_HEADS):
        for i in (0, 1):
            kv_in[g, i] = kwide[i, pl.ds(g, TOK_DEV, KV_HEADS), :].astype(BF16)

    pl.semaphore_wait(barrier, 1 + 2 * has_ahead.astype(jnp.int32) + 2 * has_behind.astype(jnp.int32))

    def remote(src, dst, send, recv, target):
        return pltpu.make_async_remote_copy(
            src_ref=src, dst_ref=dst, send_sem=send, recv_sem=recv, device_id=(target,), device_id_type=MESH
        )

    my_tok = pl.ds(pl.multiple_of(core * TOK_DEV, TOK_DEV), TOK_DEV)
    my_key = pl.ds(pl.multiple_of(WINDOW + core * TOK_DEV, TOK_DEV), TOK_DEV)
    my_back = pl.ds(pl.multiple_of(CHIP_TOK + core * TOK_DEV, TOK_DEV), TOK_DEV)
    my_row = pl.ds(pl.multiple_of(core * ROWS, ROWS), ROWS)
    other_tok = pl.ds(pl.multiple_of(WINDOW + other * TOK_DEV, TOK_DEV), TOK_DEV)
    other_row = pl.ds(pl.multiple_of(other * ROWS, ROWS), ROWS)

    def local_kv(h):
        return pltpu.make_async_copy(kv_in.at[core * MINE + h], kvb.at[h, :, my_key, :], loc_kv.at[h])

    def local_qd(h):
        return pltpu.make_async_copy(qd_in.at[core * MINE + h], qdb.at[h, :, my_row, :], loc_qd.at[h])

    def swap_kv(h):
        return remote(kv_in.at[other * MINE + h], kvb.at[h, :, my_key, :], xkv_s.at[h], xkv_r.at[h], partner)

    def swap_qd(h):
        return remote(qd_in.at[other * MINE + h], qdb.at[h, :, my_row, :], xqd_s.at[h], xqd_r.at[h], partner)

    def own_same(h):
        return remote(kv_in.at[core * MINE + h], kvb.at[h, :, my_back, :], own_s.at[h, 0], own_r.at[h, core], ahead)

    def own_cross(h):
        return remote(kv_in.at[other * MINE + h], kvb.at[h, :, my_back, :], own_s.at[h, 1], own_r.at[h, core], ahead_other)

    def came(h, j):
        tok = pl.ds(pl.multiple_of(CHIP_TOK + j * TOK_DEV, TOK_DEV), TOK_DEV)
        return remote(kvb.at[h, :, tok, :], kvb.at[h, :, tok, :], own_s.at[h, j], own_r.at[h, j], ahead)

    def relay(h, j):
        tok = pl.ds(pl.multiple_of(CHIP_TOK + j * TOK_DEV, TOK_DEV), TOK_DEV)
        to = pl.ds(pl.multiple_of(j * TOK_DEV, TOK_DEV), TOK_DEV)
        return remote(kvb.at[h, :, tok, :], kvb.at[h, :, to, :], fwd_s.at[h, j], fwd_r.at[h, j], ahead)

    def far(h, a):
        return remote(p0_out.at[h, a], p0_in.at[h, a], p0_s.at[h, a], p0_r.at[h, a], behind)

    def near(h, a):
        return remote(s_out.at[h, a], s_in.at[h, a], sum_s.at[h, a], sum_r.at[h, a], behind)

    def give_dq(h):
        return remote(dq_send.at[h], dq_got.at[h], dq_s.at[h], dq_r.at[h], partner)

    def give_dkv(h):
        return remote(dkv_send.at[h], dkv_got.at[h], dkv_s.at[h], dkv_r.at[h], partner)

    def send_own(h):
        @pl.when(has_ahead)
        def _():
            own_same(h).start()
            own_cross(h).start()

    def pass_on(h, j):
        @pl.when(has_behind)
        def _():
            came(h, j).wait_recv()

        @pl.when(has_behind & has_ahead)
        def _():
            relay(h, j).start()

    send_own(0)
    for h in range(MINE):
        local_kv(h).start()
        swap_kv(h).start()
    for i in (0, 1):
        raws[2 + i].wait()
        qwide[i] = qraw[i].astype(F32).reshape(TOK_DEV * HEADS, HEAD_WIDTH)
    for g in range(KV_HEADS):
        for i in (0, 1):
            for r in range(GROUP):
                qd_in[g, i, pl.ds(r * TOK_DEV, TOK_DEV), :] = qwide[i, pl.ds(g * GROUP + r, TOK_DEV, HEADS), :].astype(BF16)
    for h in range(MINE):
        local_qd(h).start()
        swap_qd(h).start()

    @pl.when(chip == 0)
    def _():
        kvb[:, :, pl.ds(0, WINDOW), :] = jnp.zeros((MINE, 2, WINDOW, HEAD_WIDTH), BF16)

    @pl.when(chip == 1)
    def _():
        kvb[:, :, pl.ds(0, CHIP_TOK), :] = jnp.zeros((MINE, 2, CHIP_TOK, HEAD_WIDTH), BF16)

    pass_on(0, core)
    pass_on(0, other)
    send_own(1)
    send_own(2)

    first_key = WINDOW - CHIP_TOK * chip

    def keep_dq(g, rows):
        for r in range(GROUP):
            dq_wide[pl.ds(g * GROUP + r, TOK_DEV, HEADS), :] = rows[r * TOK_DEV : (r + 1) * TOK_DEV]

    def keep_dkv(g, pair):
        for i in (0, 1):
            dkv_wide[i, pl.ds(g, TOK_DEV, KV_HEADS), :] = pair[i]

    def half(h, b):
        key_at = pl.ds(b * TOK_DEV, REACH)
        row_at = pl.ds(b * ROWS, ROWS)
        k = kvb[h, 0, key_at, :]
        v = kvb[h, 1, key_at, :]
        q = qdb[h, 0, row_at, :]
        do = qdb[h, 1, row_at, :]
        s = dot(k, q, (1, 1))
        key_pos = lax.broadcasted_iota(jnp.int32, (REACH, ROWS), 0)
        query_pos = lax.broadcasted_iota(jnp.int32, (REACH, ROWS), 1) % TOK_DEV
        distance = key_pos - query_pos
        visible = (distance > 0) & (distance <= WINDOW) & (key_pos >= first_key - b * TOK_DEV)
        s = jnp.where(visible, s, -1e30)
        top = jnp.max(s, axis=0, keepdims=True)
        e = jnp.exp((s - top) * SCALE)
        p = e * (1.0 / jnp.sum(e, axis=0, keepdims=True))
        low = p.astype(BF16)
        o = dot(v, low, (0, 0)).astype(BF16).astype(F32)
        row_dot = jnp.sum(o * do.astype(F32).T, axis=0, keepdims=True)
        gp = dot(v, do, (1, 1))
        gs = (p * (gp - row_dot)).astype(BF16)
        dv = dot(low, do, (1, 0))
        dk = dot(gs, q, (1, 0)) * SCALE
        dq = (dot(k, gs, (0, 0)) * SCALE).T
        if b == 0:
            acc[h, 0, pl.ds(0, REACH), :] = dk
            acc[h, 1, pl.ds(0, REACH), :] = dv
            acc[h, 0, pl.ds(REACH, TOK_DEV), :] = jnp.zeros((TOK_DEV, HEAD_WIDTH), F32)
            acc[h, 1, pl.ds(REACH, TOK_DEV), :] = jnp.zeros((TOK_DEV, HEAD_WIDTH), F32)
        else:
            acc[h, 0, key_at, :] += dk
            acc[h, 1, key_at, :] += dv

        @pl.when(core == b)
        def _():
            keep_dq(core * MINE + h, dq)

        @pl.when(core != b)
        def _():
            dq_send[h] = dq.astype(BF16)

    def send_far(h, a):
        @pl.when(has_far)
        def _():
            p0_out[h, a] = acc[h, :, pl.ds(a * TOK_DEV, TOK_DEV), :].astype(BF16)
            far(h, a).start()

    def add_near(h, a):
        at = pl.ds(CHIP_TOK + a * TOK_DEV, TOK_DEV)

        @pl.when(has_behind & has_ahead)
        def _():
            far(h, a).wait_recv()
            s_out[h, a] = (acc[h, :, at, :] + p0_in[h, a].astype(F32)).astype(BF16)

        @pl.when(chip == last)
        def _():
            s_out[h, a] = acc[h, :, at, :].astype(BF16)

        @pl.when(has_behind)
        def _():
            near(h, a).start()

    def finish(h, a):
        at = pl.ds(WINDOW + a * TOK_DEV, TOK_DEV)

        @pl.when(has_ahead)
        def _():
            near(h, a).wait_recv()

        @pl.when(chip == last)
        def _():
            s_in[h, a] = jnp.zeros((2, TOK_DEV, HEAD_WIDTH), BF16)

        total = acc[h, :, at, :] + s_in[h, a].astype(F32)

        @pl.when(core == a)
        def _():
            keep_dkv(core * MINE + h, total)

        @pl.when(core != a)
        def _():
            dkv_send[h] = total.astype(BF16)
            give_dkv(h).start()

    def pass_both(h):
        pass_on(h, core)
        pass_on(h, other)

    def add_both(h):
        add_near(h, 0)
        add_near(h, 1)

    def finish_both(h):
        finish(h, 0)
        finish(h, 1)

    def step(h, carry):
        local_kv(h).wait()
        local_qd(h).wait()
        swap_kv(h).wait_recv()
        swap_qd(h).wait_recv()

        @pl.when(has_far)
        def _():
            relay(h, 0).wait_recv()
            relay(h, 1).wait_recv()

        half(h, 0)
        send_far(h, 0)

        @pl.when(h == 0)
        def _():
            pass_on(1, core)

        half(h, 1)
        send_far(h, 1)
        give_dq(h).start()

        @pl.when(h == 0)
        def _():
            pass_on(1, other)
            send_own(3)

        @pl.when(h + 2 < MINE)
        def _():
            pass_both(h + 2)
            add_both(h)

        @pl.when(h == MINE - 1)
        def _():
            add_both(h - 1)

        @pl.when((h >= 1) & (h + 1 < MINE))
        def _():
            finish_both(h - 1)

        return carry

    lax.fori_loop(0, MINE, step, 0)
    add_both(MINE - 1)
    finish_both(MINE - 2)
    finish_both(MINE - 1)

    for h in range(MINE):
        give_dq(h).wait_recv()
        keep_dq(other * MINE + h, dq_got[h].astype(F32))
    dq_out[...] = dq_wide[...].astype(BF16).reshape(TOK_DEV, HEADS, HEAD_WIDTH)
    for h in range(MINE):
        give_dkv(h).wait_recv()
        keep_dkv(other * MINE + h, dkv_got[h].astype(F32))
    dk_out[...] = dkv_wide[0].astype(BF16).reshape(TOK_DEV, KV_HEADS, HEAD_WIDTH)
    dv_out[...] = dkv_wide[1].astype(BF16).reshape(TOK_DEV, KV_HEADS, HEAD_WIDTH)

    for h in range(MINE):
        swap_kv(h).wait_send()
        swap_qd(h).wait_send()
        give_dq(h).wait_send()
        give_dkv(h).wait_send()

    @pl.when(has_ahead)
    def _():
        for h in range(MINE):
            own_same(h).wait_send()
            own_cross(h).wait_send()

    @pl.when(has_behind & has_ahead)
    def _():
        for h in range(MINE):
            relay(h, 0).wait_send()
            relay(h, 1).wait_send()

    @pl.when(has_far)
    def _():
        for h in range(MINE):
            far(h, 0).wait_send()
            far(h, 1).wait_send()

    @pl.when(has_behind)
    def _():
        for h in range(MINE):
            near(h, 0).wait_send()
            near(h, 1).wait_send()


def body(n, queries, keys, values, d_out):
    dma = pltpu.SemaphoreType.DMA
    wide = (TOK_DEV, HEADS, HEAD_WIDTH)
    slim = (TOK_DEV, KV_HEADS, HEAD_WIDTH)
    return pl.pallas_call(
        functools.partial(kernel, n),
        out_shape=(
            jax.ShapeDtypeStruct(wide, BF16),
            jax.ShapeDtypeStruct(slim, BF16),
            jax.ShapeDtypeStruct(slim, BF16),
        ),
        in_specs=[pl.BlockSpec(memory_space=pltpu.HBM)] * 4,
        out_specs=(pl.BlockSpec(memory_space=pltpu.VMEM),) * 3,
        scratch_shapes=[
            pltpu.VMEM((2,) + slim, BF16),
            pltpu.VMEM((2,) + wide, BF16),
            pltpu.VMEM((2, TOK_DEV * KV_HEADS, HEAD_WIDTH), F32),
            pltpu.VMEM((2, TOK_DEV * HEADS, HEAD_WIDTH), F32),
            pltpu.VMEM((KV_HEADS, 2, TOK_DEV, HEAD_WIDTH), BF16),
            pltpu.VMEM((KV_HEADS, 2, ROWS, HEAD_WIDTH), BF16),
            pltpu.VMEM((TOK_DEV * HEADS, HEAD_WIDTH), F32),
            pltpu.VMEM((2, TOK_DEV * KV_HEADS, HEAD_WIDTH), F32),
            pltpu.VMEM((MINE, 2, SPAN, HEAD_WIDTH), BF16),
            pltpu.VMEM((MINE, 2, 2 * ROWS, HEAD_WIDTH), BF16),
            pltpu.VMEM((MINE, 2, SPAN, HEAD_WIDTH), F32),
            pltpu.VMEM((MINE, 2, 2, TOK_DEV, HEAD_WIDTH), BF16),
            pltpu.VMEM((MINE, 2, 2, TOK_DEV, HEAD_WIDTH), BF16),
            pltpu.VMEM((MINE, 2, 2, TOK_DEV, HEAD_WIDTH), BF16),
            pltpu.VMEM((MINE, 2, 2, TOK_DEV, HEAD_WIDTH), BF16),
            pltpu.VMEM((MINE, ROWS, HEAD_WIDTH), BF16),
            pltpu.VMEM((MINE, 2, TOK_DEV, HEAD_WIDTH), BF16),
            pltpu.VMEM((MINE, ROWS, HEAD_WIDTH), BF16),
            pltpu.VMEM((MINE, 2, TOK_DEV, HEAD_WIDTH), BF16),
            dma((4,)),
        ]
        + [dma((MINE,))] * 6
        + [dma((MINE, 2))] * 8
        + [dma((MINE,))] * 4,
        compiler_params=pltpu.CompilerParams(collective_id=0, has_side_effects=True, vmem_limit_bytes=60 * 1024 * 1024),
    )(queries, keys, values, d_out)


def solution(mesh):
    placed = P("ctx", None, None)
    return jax.shard_map(
        functools.partial(body, mesh.shape["ctx"]),
        mesh=mesh,
        in_specs=(placed,) * 4,
        out_specs=(placed,) * 3,
        check_vma=False,
    )
```

```python
import functools

import jax
import jax.numpy as jnp
from jax import lax
from jax.experimental import pallas as pl
from jax.experimental.pallas import tpu as pltpu
from jax.sharding import PartitionSpec as P

HEADS = 16
KV_HEADS = 8
HEAD_WIDTH = 128
WINDOW = 512
TOK_DEV = 128
GROUP = HEADS // KV_HEADS
CHIP_TOK = 2 * TOK_DEV
SPAN = WINDOW + CHIP_TOK
REACH = WINDOW + TOK_DEV
ROWS = GROUP * TOK_DEV
MINE = KV_HEADS // 2

MESH = pl.DeviceIdType.MESH
SCALE = 168.0 ** (-0.5)
F32 = jnp.float32
BF16 = jnp.bfloat16


def dot(a, b, contract):
    return lax.dot_general(a, b, ((contract[:1], contract[1:]), ((), ())), preferred_element_type=F32)


def kernel(
    n, q_in, k_in, v_in, do_in, dq_out, dk_out, dv_out,
    kraw, qraw, kwide, qwide, kv_in, qd_in, dq_wide, dkv_wide,
    kvb, qdb, acc, p0_out, p0_in, s_out, s_in, dq_send, dq_got, dkv_got,
    raw_s, loc_kv, loc_qd, xkv_s, xkv_r, xqd_s, xqd_r, own_s, own_r, fwd_s, fwd_r,
    p0_s, p0_r, sum_s, sum_r, dq_s, dq_r, dkv_s, dkv_r,
):
    me = lax.axis_index("ctx")
    chip = me // 2
    core = me % 2
    other = 1 - core
    partner = chip * 2 + other
    ahead = (me + 2) % n
    ahead_other = (partner + 2) % n
    behind = (me + n - 2) % n
    behind_other = (partner + n - 2) % n
    last = n // 2 - 1
    has_ahead = chip < last
    has_behind = chip > 0
    has_far = chip > 1

    barrier = pltpu.get_barrier_semaphore()

    def greet(*peers):
        for peer in peers:
            pl.semaphore_signal(barrier, inc=1, device_id=(peer,), device_id_type=MESH)

    greet(partner)
    pl.when(has_behind)(lambda: greet(behind, behind_other))

    raws = [
        pltpu.make_async_copy(src, dst, raw_s.at[i])
        for i, (src, dst) in enumerate(
            ((k_in, kraw.at[0]), (v_in, kraw.at[1]), (q_in, qraw.at[0]), (do_in, qraw.at[1]))
        )
    ]
    for copy in raws:
        copy.start()
    for i in (0, 1):
        raws[i].wait()
        kwide[i] = kraw[i].astype(F32).reshape(TOK_DEV * KV_HEADS, HEAD_WIDTH)
    for g in range(KV_HEADS):
        for i in (0, 1):
            kv_in[g, i] = kwide[i, pl.ds(g, TOK_DEV, KV_HEADS), :].astype(BF16)

    pl.semaphore_wait(barrier, 1 + 2 * has_ahead.astype(jnp.int32))

    def remote(src, dst, send, recv, target):
        return pltpu.make_async_remote_copy(
            src_ref=src, dst_ref=dst, send_sem=send, recv_sem=recv, device_id=(target,), device_id_type=MESH
        )

    my_tok = pl.ds(pl.multiple_of(core * TOK_DEV, TOK_DEV), TOK_DEV)
    my_key = pl.ds(pl.multiple_of(WINDOW + core * TOK_DEV, TOK_DEV), TOK_DEV)
    my_back = pl.ds(pl.multiple_of(CHIP_TOK + core * TOK_DEV, TOK_DEV), TOK_DEV)
    my_row = pl.ds(pl.multiple_of(core * ROWS, ROWS), ROWS)
    other_tok = pl.ds(pl.multiple_of(WINDOW + other * TOK_DEV, TOK_DEV), TOK_DEV)
    other_row = pl.ds(pl.multiple_of(other * ROWS, ROWS), ROWS)

    def local_kv(h):
        return pltpu.make_async_copy(kv_in.at[core * MINE + h], kvb.at[h, :, my_key, :], loc_kv.at[h])

    def local_qd(h):
        return pltpu.make_async_copy(qd_in.at[core * MINE + h], qdb.at[h, :, my_row, :], loc_qd.at[h])

    def swap_kv(h):
        return remote(kv_in.at[other * MINE + h], kvb.at[h, :, my_key, :], xkv_s.at[h], xkv_r.at[h], partner)

    def swap_qd(h):
        return remote(qd_in.at[other * MINE + h], qdb.at[h, :, my_row, :], xqd_s.at[h], xqd_r.at[h], partner)

    def own_same(h):
        return remote(kv_in.at[core * MINE + h], kvb.at[h, :, my_back, :], own_s.at[h, 0], own_r.at[h, core], ahead)

    def own_cross(h):
        return remote(kv_in.at[other * MINE + h], kvb.at[h, :, my_back, :], own_s.at[h, 1], own_r.at[h, core], ahead_other)

    def came(h, j):
        tok = pl.ds(pl.multiple_of(CHIP_TOK + j * TOK_DEV, TOK_DEV), TOK_DEV)
        return remote(kvb.at[h, :, tok, :], kvb.at[h, :, tok, :], own_s.at[h, j], own_r.at[h, j], ahead)

    def relay(h, j):
        tok = pl.ds(pl.multiple_of(CHIP_TOK + j * TOK_DEV, TOK_DEV), TOK_DEV)
        to = pl.ds(pl.multiple_of(j * TOK_DEV, TOK_DEV), TOK_DEV)
        return remote(kvb.at[h, :, tok, :], kvb.at[h, :, to, :], fwd_s.at[h, j], fwd_r.at[h, j], ahead)

    def far(h, a):
        return remote(p0_out.at[h, a], p0_in.at[h, a], p0_s.at[h, a], p0_r.at[h, a], behind)

    def near(h, a):
        g = core * MINE + h
        return remote(s_out.at[h, a], s_in.at[g], sum_s.at[h, a], sum_r.at[g], behind - core + a)

    def near_in(g):
        return remote(s_in.at[g], s_in.at[g], sum_s.at[0, 0], sum_r.at[g], behind)

    def give_dq(h):
        return remote(dq_send.at[h], dq_got.at[h], dq_s.at[h], dq_r.at[h], partner)

    def give_dkv(h):
        return remote(acc.at[h, :, other_tok, :], dkv_got.at[h], dkv_s.at[h], dkv_r.at[h], partner)

    def send_own(h):
        @pl.when(has_ahead)
        def _():
            own_same(h).start()
            own_cross(h).start()

    def pass_on(h, j):
        @pl.when(has_behind)
        def _():
            came(h, j).wait_recv()

        @pl.when(has_behind & has_ahead)
        def _():
            relay(h, j).start()

    def pass_both(h):
        pass_on(h, core)
        pass_on(h, other)

    send_own(0)

    @pl.when(chip == 1)
    def _():
        for h in range(1, MINE):
            send_own(h)

    for h in range(MINE):
        local_kv(h).start()
        swap_kv(h).start()
    for i in (0, 1):
        raws[2 + i].wait()
        qwide[i] = qraw[i].astype(F32).reshape(TOK_DEV * HEADS, HEAD_WIDTH)
    for g in range(KV_HEADS):
        for i in (0, 1):
            for r in range(GROUP):
                qd_in[g, i, pl.ds(r * TOK_DEV, TOK_DEV), :] = qwide[i, pl.ds(g * GROUP + r, TOK_DEV, HEADS), :].astype(BF16)
    for h in range(MINE):
        local_qd(h).start()
        swap_qd(h).start()

    @pl.when(chip == 0)
    def _():
        kvb[:, :, pl.ds(0, WINDOW), :] = jnp.zeros((MINE, 2, WINDOW, HEAD_WIDTH), BF16)

    @pl.when(chip == 1)
    def _():
        kvb[:, :, pl.ds(0, CHIP_TOK), :] = jnp.zeros((MINE, 2, CHIP_TOK, HEAD_WIDTH), BF16)

    pass_both(0)

    @pl.when(chip != 1)
    def _():
        send_own(1)
        send_own(2)

    pass_both(1)

    @pl.when(chip != 1)
    def _():
        send_own(3)

    @pl.when(chip == 2)
    def _():
        pass_both(2)
        pass_both(3)

    first_key = WINDOW - CHIP_TOK * chip

    def keep_dq(g, rows):
        for r in range(GROUP):
            dq_wide[pl.ds(g * GROUP + r, TOK_DEV, HEADS), :] = rows[r * TOK_DEV : (r + 1) * TOK_DEV]

    def half(h, b):
        key_at = pl.ds(b * TOK_DEV, REACH)
        row_at = pl.ds(b * ROWS, ROWS)
        k = kvb[h, 0, key_at, :]
        v = kvb[h, 1, key_at, :]
        q = qdb[h, 0, row_at, :]
        do = qdb[h, 1, row_at, :]
        s = dot(k, q, (1, 1))
        key_pos = lax.broadcasted_iota(jnp.int32, (REACH, ROWS), 0)
        query_pos = lax.broadcasted_iota(jnp.int32, (REACH, ROWS), 1) % TOK_DEV
        distance = key_pos - query_pos
        visible = (distance > 0) & (distance <= WINDOW) & (key_pos >= first_key - b * TOK_DEV)
        s = jnp.where(visible, s, -1e30)
        top = jnp.max(s, axis=0, keepdims=True)
        e = jnp.exp((s - top) * SCALE)
        p = e * (1.0 / jnp.sum(e, axis=0, keepdims=True))
        low = p.astype(BF16)
        o = dot(v, low, (0, 0)).astype(BF16).astype(F32)
        row_dot = jnp.sum(o * do.astype(F32).T, axis=0, keepdims=True)
        gp = dot(v, do, (1, 1))
        gs = (p * (gp - row_dot)).astype(BF16)
        dv = dot(low, do, (1, 0))
        dk = dot(gs, q, (1, 0)) * SCALE
        dq = (dot(k, gs, (0, 0)) * SCALE).T
        if b == 0:
            acc[h, 0, pl.ds(0, REACH), :] = dk
            acc[h, 1, pl.ds(0, REACH), :] = dv
            acc[h, 0, pl.ds(REACH, TOK_DEV), :] = jnp.zeros((TOK_DEV, HEAD_WIDTH), F32)
            acc[h, 1, pl.ds(REACH, TOK_DEV), :] = jnp.zeros((TOK_DEV, HEAD_WIDTH), F32)
        else:
            acc[h, 0, key_at, :] += dk
            acc[h, 1, key_at, :] += dv

        @pl.when(core == b)
        def _():
            keep_dq(core * MINE + h, dq)

        @pl.when(core != b)
        def _():
            dq_send[h] = dq.astype(BF16)

    def send_far(h, a):
        @pl.when(has_far)
        def _():
            p0_out[h, a] = acc[h, :, pl.ds(a * TOK_DEV, TOK_DEV), :].astype(BF16)
            far(h, a).start()

    def add_near(h, a):
        at = pl.ds(CHIP_TOK + a * TOK_DEV, TOK_DEV)

        @pl.when(has_behind & has_ahead)
        def _():
            far(h, a).wait_recv()
            s_out[h, a] = (acc[h, :, at, :] + p0_in[h, a].astype(F32)).astype(BF16)

        @pl.when(chip == last)
        def _():
            s_out[h, a] = acc[h, :, at, :].astype(BF16)

        @pl.when(has_behind)
        def _():
            near(h, a).start()

    def finish(g, own):
        @pl.when(has_ahead)
        def _():
            near_in(g).wait_recv()

        @pl.when(chip == last)
        def _():
            s_in[g] = jnp.zeros((2, TOK_DEV, HEAD_WIDTH), BF16)

        total = own + s_in[g].astype(F32)
        for i in (0, 1):
            dkv_wide[i, pl.ds(g, TOK_DEV, KV_HEADS), :] = total[i]

    def finish_both(h):
        give_dq(h).wait_recv()
        keep_dq(other * MINE + h, dq_got[h].astype(F32))
        give_dkv(h).wait_recv()
        finish(core * MINE + h, acc[h, :, my_key, :])
        finish(other * MINE + h, dkv_got[h])

    def add_both(h):
        add_near(h, 0)
        add_near(h, 1)

    def step(h, carry):
        local_kv(h).wait()
        local_qd(h).wait()
        swap_kv(h).wait_recv()
        swap_qd(h).wait_recv()

        @pl.when(has_far)
        def _():
            relay(h, 0).wait_recv()
            relay(h, 1).wait_recv()

        half(h, 0)
        send_far(h, 0)

        half(h, 1)
        send_far(h, 1)
        give_dq(h).start()
        give_dkv(h).start()

        @pl.when((h + 2 < MINE) & (chip != 2))
        def _():
            pass_both(h + 2)

        @pl.when(h + 2 < MINE)
        def _():
            add_both(h)

        @pl.when(h == MINE - 1)
        def _():
            add_both(h - 1)

        @pl.when((h >= 1) & (h + 1 < MINE))
        def _():
            finish_both(h - 1)

        return carry

    lax.fori_loop(0, MINE, step, 0)
    add_both(MINE - 1)
    finish_both(MINE - 2)
    give_dq(MINE - 1).wait_recv()
    keep_dq(other * MINE + MINE - 1, dq_got[MINE - 1].astype(F32))
    dq_out[...] = dq_wide[...].astype(BF16).reshape(TOK_DEV, HEADS, HEAD_WIDTH)
    give_dkv(MINE - 1).wait_recv()
    finish(core * MINE + MINE - 1, acc[MINE - 1, :, my_key, :])
    finish(other * MINE + MINE - 1, dkv_got[MINE - 1])
    dk_out[...] = dkv_wide[0].astype(BF16).reshape(TOK_DEV, KV_HEADS, HEAD_WIDTH)
    dv_out[...] = dkv_wide[1].astype(BF16).reshape(TOK_DEV, KV_HEADS, HEAD_WIDTH)

    for h in range(MINE):
        swap_kv(h).wait_send()
        swap_qd(h).wait_send()
        give_dq(h).wait_send()
        give_dkv(h).wait_send()

    @pl.when(has_ahead)
    def _():
        for h in range(MINE):
            own_same(h).wait_send()
            own_cross(h).wait_send()

    @pl.when(has_behind & has_ahead)
    def _():
        for h in range(MINE):
            relay(h, 0).wait_send()
            relay(h, 1).wait_send()

    @pl.when(has_far)
    def _():
        for h in range(MINE):
            far(h, 0).wait_send()
            far(h, 1).wait_send()

    @pl.when(has_behind)
    def _():
        for h in range(MINE):
            near(h, 0).wait_send()
            near(h, 1).wait_send()


def body(n, queries, keys, values, d_out):
    dma = pltpu.SemaphoreType.DMA
    wide = (TOK_DEV, HEADS, HEAD_WIDTH)
    slim = (TOK_DEV, KV_HEADS, HEAD_WIDTH)
    return pl.pallas_call(
        functools.partial(kernel, n),
        out_shape=(
            jax.ShapeDtypeStruct(wide, BF16),
            jax.ShapeDtypeStruct(slim, BF16),
            jax.ShapeDtypeStruct(slim, BF16),
        ),
        in_specs=[pl.BlockSpec(memory_space=pltpu.HBM)] * 4,
        out_specs=(pl.BlockSpec(memory_space=pltpu.VMEM),) * 3,
        scratch_shapes=[
            pltpu.VMEM((2,) + slim, BF16),
            pltpu.VMEM((2,) + wide, BF16),
            pltpu.VMEM((2, TOK_DEV * KV_HEADS, HEAD_WIDTH), F32),
            pltpu.VMEM((2, TOK_DEV * HEADS, HEAD_WIDTH), F32),
            pltpu.VMEM((KV_HEADS, 2, TOK_DEV, HEAD_WIDTH), BF16),
            pltpu.VMEM((KV_HEADS, 2, ROWS, HEAD_WIDTH), BF16),
            pltpu.VMEM((TOK_DEV * HEADS, HEAD_WIDTH), F32),
            pltpu.VMEM((2, TOK_DEV * KV_HEADS, HEAD_WIDTH), F32),
            pltpu.VMEM((MINE, 2, SPAN, HEAD_WIDTH), BF16),
            pltpu.VMEM((MINE, 2, 2 * ROWS, HEAD_WIDTH), BF16),
            pltpu.VMEM((MINE, 2, SPAN, HEAD_WIDTH), F32),
            pltpu.VMEM((MINE, 2, 2, TOK_DEV, HEAD_WIDTH), BF16),
            pltpu.VMEM((MINE, 2, 2, TOK_DEV, HEAD_WIDTH), BF16),
            pltpu.VMEM((MINE, 2, 2, TOK_DEV, HEAD_WIDTH), BF16),
            pltpu.VMEM((KV_HEADS, 2, TOK_DEV, HEAD_WIDTH), BF16),
            pltpu.VMEM((MINE, ROWS, HEAD_WIDTH), BF16),
            pltpu.VMEM((MINE, ROWS, HEAD_WIDTH), BF16),
            pltpu.VMEM((MINE, 2, TOK_DEV, HEAD_WIDTH), F32),
            dma((4,)),
        ]
        + [dma((MINE,))] * 6
        + [dma((MINE, 2))] * 7
        + [dma((KV_HEADS,))]
        + [dma((MINE,))] * 4,
        compiler_params=pltpu.CompilerParams(collective_id=0, has_side_effects=True, vmem_limit_bytes=48000 * 1024),
    )(*(pltpu.with_memory_space_constraint(a, pltpu.HBM) for a in (queries, keys, values, d_out)))


def solution(mesh):
    placed = P("ctx", None, None)
    return jax.shard_map(
        functools.partial(body, mesh.shape["ctx"]),
        mesh=mesh,
        in_specs=(placed,) * 4,
        out_specs=(placed,) * 3,
        check_vma=False,
    )
```

```python
import functools

import jax
import jax.numpy as jnp
from jax import lax
from jax.experimental import pallas as pl
from jax.experimental.pallas import tpu as pltpu
from jax.sharding import PartitionSpec as P

HEADS = 16
KV_HEADS = 8
HEAD_WIDTH = 128
WINDOW = 512
TOK_DEV = 128
GROUP = HEADS // KV_HEADS
CHIP_TOK = 2 * TOK_DEV
SPAN = WINDOW + CHIP_TOK
REACH = WINDOW + TOK_DEV
ROWS = GROUP * TOK_DEV
MINE = KV_HEADS // 2
ROUND = 1
LAST = MINE - 1
RING = 4

MESH = pl.DeviceIdType.MESH
SCALE = 168.0 ** (-0.5)
F32 = jnp.float32
BF16 = jnp.bfloat16


def dot(a, b, contract):
    return lax.dot_general(a, b, ((contract[:1], contract[1:]), ((), ())), preferred_element_type=F32)


def kernel(
    n, q_in, k_in, v_in, do_in, dq_out, dk_out, dv_out,
    kraw, qraw, kwide, qwide, kv_in, qd_in, dq_wide, dkv_wide,
    kvb, qdb, acc, p0_out, p0_in, s_out, s_in, dq_send, dq_got, dkv_got, rb, cb, pc_in,
    raw_s, loc_kv, loc_qd, xkv_s, xkv_r, xqd_s, xqd_r, own_s, own_r, fwd_s, fwd_r,
    p0_s, p0_r, sum_s, sum_r, dq_s, dq_r, dkv_s, dkv_r,
    b1_s, b1_r, b2_s, c1_s, c1_r, c2_s, c2_r,
):
    me = lax.axis_index("ctx")
    chip = me // 2
    core = me % 2
    other = 1 - core
    partner = chip * 2 + other
    ahead = (me + 2) % n
    ahead_other = (partner + 2) % n
    behind = (me + n - 2) % n
    behind_other = (partner + n - 2) % n
    last = n // 2 - 1
    has_ahead = chip < last
    has_behind = chip > 0
    has_far = chip > 1
    row = chip // RING * RING
    up = row + (chip + 1) % RING
    down = row + (chip + RING - 1) % RING
    has_two = chip + 2 <= last
    up_two = up + 2 <= last
    down_two = down >= 2

    def ring_of(c, d):
        return c // RING * RING + (c + d) % RING

    def dev(c, k):
        return c * 2 + k

    barrier = pltpu.get_barrier_semaphore()

    def greet(*peers):
        for peer in peers:
            pl.semaphore_signal(barrier, inc=1, device_id=(peer,), device_id_type=MESH)

    greet(partner)
    greet(dev(up, 0), dev(up, 1), dev(down, core))
    pl.when(has_behind)(lambda: greet(behind, behind_other))
    pl.when(has_far)(lambda: greet(dev(ring_of(chip - 2, RING - 1), core)))
    pl.when(has_two)(lambda: greet(dev(ring_of(chip + 2, 1), 0), dev(ring_of(chip + 2, 1), 1)))

    raws = [
        pltpu.make_async_copy(src, dst, raw_s.at[i])
        for i, (src, dst) in enumerate(
            ((k_in, kraw.at[0]), (v_in, kraw.at[1]), (q_in, qraw.at[0]), (do_in, qraw.at[1]))
        )
    ]
    for copy in raws:
        copy.start()
    for i in (0, 1):
        raws[i].wait()
        kwide[i] = kraw[i].astype(F32).reshape(TOK_DEV * KV_HEADS, HEAD_WIDTH)
    for g in range(KV_HEADS):
        for i in (0, 1):
            kv_in[g, i] = kwide[i, pl.ds(g, TOK_DEV, KV_HEADS), :].astype(BF16)

    known = 2 * has_ahead.astype(jnp.int32) + up_two.astype(jnp.int32) + 2 * down_two.astype(jnp.int32)
    pl.semaphore_wait(barrier, 4 + known)

    def remote(src, dst, send, recv, target):
        return pltpu.make_async_remote_copy(
            src_ref=src, dst_ref=dst, send_sem=send, recv_sem=recv, device_id=(target,), device_id_type=MESH
        )

    my_tok = pl.ds(pl.multiple_of(core * TOK_DEV, TOK_DEV), TOK_DEV)
    my_key = pl.ds(pl.multiple_of(WINDOW + core * TOK_DEV, TOK_DEV), TOK_DEV)
    my_back = pl.ds(pl.multiple_of(CHIP_TOK + core * TOK_DEV, TOK_DEV), TOK_DEV)
    my_row = pl.ds(pl.multiple_of(core * ROWS, ROWS), ROWS)
    other_tok = pl.ds(pl.multiple_of(WINDOW + other * TOK_DEV, TOK_DEV), TOK_DEV)
    other_row = pl.ds(pl.multiple_of(other * ROWS, ROWS), ROWS)

    def local_kv(h):
        return pltpu.make_async_copy(kv_in.at[core * MINE + h], kvb.at[h, :, my_key, :], loc_kv.at[h])

    def local_qd(h):
        return pltpu.make_async_copy(qd_in.at[core * MINE + h], qdb.at[h, :, my_row, :], loc_qd.at[h])

    def swap_kv(h):
        return remote(kv_in.at[other * MINE + h], kvb.at[h, :, my_key, :], xkv_s.at[h], xkv_r.at[h], partner)

    def swap_qd(h):
        return remote(qd_in.at[other * MINE + h], qdb.at[h, :, my_row, :], xqd_s.at[h], xqd_r.at[h], partner)

    def own_same(h):
        return remote(kv_in.at[core * MINE + h], kvb.at[h, :, my_back, :], own_s.at[h, 0], own_r.at[h, core], ahead)

    def own_cross(h):
        return remote(kv_in.at[other * MINE + h], kvb.at[h, :, my_back, :], own_s.at[h, 1], own_r.at[h, core], ahead_other)

    def came(h, j):
        tok = pl.ds(pl.multiple_of(CHIP_TOK + j * TOK_DEV, TOK_DEV), TOK_DEV)
        return remote(kvb.at[h, :, tok, :], kvb.at[h, :, tok, :], own_s.at[h, j], own_r.at[h, j], ahead)

    def relay(h, j):
        tok = pl.ds(pl.multiple_of(CHIP_TOK + j * TOK_DEV, TOK_DEV), TOK_DEV)
        to = pl.ds(pl.multiple_of(j * TOK_DEV, TOK_DEV), TOK_DEV)
        return remote(kvb.at[h, :, tok, :], kvb.at[h, :, to, :], fwd_s.at[h, j], fwd_r.at[h, j], ahead)

    def far(h, a):
        return remote(p0_out.at[h, a], p0_in.at[h, a], p0_s.at[h, a], p0_r.at[h, a], behind)

    def near(h, a):
        g = core * MINE + h
        return remote(s_out.at[h, a], s_in.at[g], sum_s.at[h, a], sum_r.at[g], behind - core + a)

    def near_in(g):
        return remote(s_in.at[g], s_in.at[g], sum_s.at[0, 0], sum_r.at[g], behind)

    def give_dq(h):
        return remote(dq_send.at[h], dq_got.at[h], dq_s.at[h], dq_r.at[h], partner)

    def give_dkv(h):
        return remote(acc.at[h, :, other_tok, :], dkv_got.at[h], dkv_s.at[h], dkv_r.at[h], partner)

    def round_same():
        return remote(kv_in.at[core * MINE + ROUND], rb.at[:, my_tok, :], b1_s.at[0], b1_r.at[core], dev(down, core))

    def round_cross():
        return remote(kv_in.at[other * MINE + ROUND], rb.at[:, my_tok, :], b1_s.at[1], b1_r.at[core], dev(down, other))

    def round_on(j):
        tok = pl.ds(pl.multiple_of(j * TOK_DEV, TOK_DEV), TOK_DEV)
        return remote(rb.at[:, tok, :], kvb.at[ROUND, :, tok, :], b2_s.at[j], fwd_r.at[ROUND, j], dev(up + 2, core))

    def round_came(j):
        tok = pl.ds(pl.multiple_of(j * TOK_DEV, TOK_DEV), TOK_DEV)
        return remote(rb.at[:, tok, :], rb.at[:, tok, :], b2_s.at[j], b1_r.at[j], ahead)

    def back(a):
        return remote(p0_out.at[LAST, a], cb.at[a], c1_s.at[a], c1_r.at[a], dev(up, core))

    def back_on(a):
        return remote(cb.at[a], pc_in.at[core], c2_s.at[a], c2_r.at[core], dev(down - 2, a))

    def back_came(k):
        return remote(pc_in.at[k], pc_in.at[k], c2_s.at[0], c2_r.at[k], ahead)

    def send_own(h):
        @pl.when(has_ahead)
        def _():
            own_same(h).start()
            own_cross(h).start()

    def pass_on(h, j):
        @pl.when(has_behind)
        def _():
            came(h, j).wait_recv()

        @pl.when(has_behind & has_ahead)
        def _():
            relay(h, j).start()

    def pass_both(h):
        pass_on(h, core)
        pass_on(h, other)

    send_own(0)

    @pl.when(has_two)
    def _():
        round_same().start()
        round_cross().start()

    @pl.when(chip == 1)
    def _():
        for h in range(1, MINE):
            send_own(h)

    for h in range(MINE):
        local_kv(h).start()
        swap_kv(h).start()
    for i in (0, 1):
        raws[2 + i].wait()
        qwide[i] = qraw[i].astype(F32).reshape(TOK_DEV * HEADS, HEAD_WIDTH)
    for g in range(KV_HEADS):
        for i in (0, 1):
            for r in range(GROUP):
                qd_in[g, i, pl.ds(r * TOK_DEV, TOK_DEV), :] = qwide[i, pl.ds(g * GROUP + r, TOK_DEV, HEADS), :].astype(BF16)
    for h in range(MINE):
        local_qd(h).start()
        swap_qd(h).start()

    @pl.when(chip == 0)
    def _():
        kvb[:, :, pl.ds(0, WINDOW), :] = jnp.zeros((MINE, 2, WINDOW, HEAD_WIDTH), BF16)

    @pl.when(chip == 1)
    def _():
        kvb[:, :, pl.ds(0, CHIP_TOK), :] = jnp.zeros((MINE, 2, CHIP_TOK, HEAD_WIDTH), BF16)

    pass_both(0)

    @pl.when(chip != 1)
    def _():
        for h in range(1, MINE):
            send_own(h)

    @pl.when(up_two)
    def _():
        for j in (core, other):
            round_came(j).wait_recv()
            round_on(j).start()

    @pl.when(chip == 2)
    def _():
        pass_both(2)
        pass_both(3)

    first_key = WINDOW - CHIP_TOK * chip

    def keep_dq(g, rows):
        for r in range(GROUP):
            dq_wide[pl.ds(g * GROUP + r, TOK_DEV, HEADS), :] = rows[r * TOK_DEV : (r + 1) * TOK_DEV]

    def half(h, b):
        key_at = pl.ds(b * TOK_DEV, REACH)
        row_at = pl.ds(b * ROWS, ROWS)
        k = kvb[h, 0, key_at, :]
        v = kvb[h, 1, key_at, :]
        q = qdb[h, 0, row_at, :]
        do = qdb[h, 1, row_at, :]
        s = dot(k, q, (1, 1))
        key_pos = lax.broadcasted_iota(jnp.int32, (REACH, ROWS), 0)
        query_pos = lax.broadcasted_iota(jnp.int32, (REACH, ROWS), 1) % TOK_DEV
        distance = key_pos - query_pos
        visible = (distance > 0) & (distance <= WINDOW) & (key_pos >= first_key - b * TOK_DEV)
        s = jnp.where(visible, s, -1e30)
        top = jnp.max(s, axis=0, keepdims=True)
        e = jnp.exp((s - top) * SCALE)
        p = e * (1.0 / jnp.sum(e, axis=0, keepdims=True))
        low = p.astype(BF16)
        o = dot(v, low, (0, 0)).astype(BF16).astype(F32)
        row_dot = jnp.sum(o * do.astype(F32).T, axis=0, keepdims=True)
        gp = dot(v, do, (1, 1))
        gs = (p * (gp - row_dot)).astype(BF16)
        dv = dot(low, do, (1, 0))
        dk = dot(gs, q, (1, 0)) * SCALE
        dq = (dot(k, gs, (0, 0)) * SCALE).T
        if b == 0:
            acc[h, 0, pl.ds(0, REACH), :] = dk
            acc[h, 1, pl.ds(0, REACH), :] = dv
            acc[h, 0, pl.ds(REACH, TOK_DEV), :] = jnp.zeros((TOK_DEV, HEAD_WIDTH), F32)
            acc[h, 1, pl.ds(REACH, TOK_DEV), :] = jnp.zeros((TOK_DEV, HEAD_WIDTH), F32)
        else:
            acc[h, 0, key_at, :] += dk
            acc[h, 1, key_at, :] += dv

        @pl.when(core == b)
        def _():
            keep_dq(core * MINE + h, dq)

        @pl.when(core != b)
        def _():
            dq_send[h] = dq.astype(BF16)

    def send_far(h, a):
        @pl.when(has_far)
        def _():
            p0_out[h, a] = acc[h, :, pl.ds(a * TOK_DEV, TOK_DEV), :].astype(BF16)

        @pl.when(has_far & (h < LAST))
        def _():
            far(h, a).start()

        @pl.when(has_far & (h == LAST))
        def _():
            back(a).start()

    def add_near(h, a):
        at = pl.ds(CHIP_TOK + a * TOK_DEV, TOK_DEV)

        @pl.when(has_behind & has_ahead & (h < LAST))
        def _():
            far(h, a).wait_recv()
            s_out[h, a] = (acc[h, :, at, :] + p0_in[h, a].astype(F32)).astype(BF16)

        @pl.when((chip == last) | (h == LAST))
        def _():
            s_out[h, a] = acc[h, :, at, :].astype(BF16)

        @pl.when(has_behind)
        def _():
            near(h, a).start()

    def finish(g, own):
        @pl.when(has_ahead)
        def _():
            near_in(g).wait_recv()

        @pl.when(chip == last)
        def _():
            s_in[g] = jnp.zeros((2, TOK_DEV, HEAD_WIDTH), BF16)

        total = own + s_in[g].astype(F32)
        for i in (0, 1):
            dkv_wide[i, pl.ds(g, TOK_DEV, KV_HEADS), :] = total[i]

    def finish_both(h):
        give_dkv(h).wait_recv()
        finish(core * MINE + h, acc[h, :, my_key, :])
        finish(other * MINE + h, dkv_got[h])

    def add_both(h):
        add_near(h, 0)
        add_near(h, 1)

    def step(h, carry):
        local_kv(h).wait()
        local_qd(h).wait()
        swap_kv(h).wait_recv()
        swap_qd(h).wait_recv()

        @pl.when(has_far)
        def _():
            relay(h, 0).wait_recv()
            relay(h, 1).wait_recv()

        @pl.when(has_behind & (h == ROUND))
        def _():
            came(ROUND, 0).wait_recv()
            came(ROUND, 1).wait_recv()

        half(h, 0)
        send_far(h, 0)

        half(h, 1)
        send_far(h, 1)
        give_dq(h).start()
        give_dkv(h).start()

        @pl.when((h == 1) & (chip != 2))
        def _():
            pass_both(2)

        @pl.when(h == 1)
        def _():
            add_both(0)

        @pl.when((h == 1) & (chip != 2))
        def _():
            pass_both(3)

        @pl.when(h == 1)
        def _():
            add_both(1)

        @pl.when(h == 2)
        def _():
            finish_both(0)

        return carry

    lax.fori_loop(0, MINE, step, 0)
    add_both(LAST)
    add_both(2)

    @pl.when(down_two)
    def _():
        for a in (0, 1):
            back(a).wait_recv()
            back_on(a).start()

    finish_both(1)
    for h in range(MINE):
        give_dq(h).wait_recv()
        keep_dq(other * MINE + h, dq_got[h].astype(F32))
    dq_out[...] = dq_wide[...].astype(BF16).reshape(TOK_DEV, HEADS, HEAD_WIDTH)
    finish_both(2)
    give_dkv(LAST).wait_recv()

    @pl.when(has_two)
    def _():
        back_came(0).wait_recv()
        back_came(1).wait_recv()

    @pl.when(chip + 2 > last)
    def _():
        pc_in[...] = jnp.zeros_like(pc_in)

    finish(core * MINE + LAST, acc[LAST, :, my_key, :] + pc_in[core].astype(F32))
    finish(other * MINE + LAST, dkv_got[LAST] + pc_in[other].astype(F32))
    dk_out[...] = dkv_wide[0].astype(BF16).reshape(TOK_DEV, KV_HEADS, HEAD_WIDTH)
    dv_out[...] = dkv_wide[1].astype(BF16).reshape(TOK_DEV, KV_HEADS, HEAD_WIDTH)

    for h in range(MINE):
        swap_kv(h).wait_send()
        swap_qd(h).wait_send()
        give_dq(h).wait_send()
        give_dkv(h).wait_send()

    @pl.when(has_ahead)
    def _():
        for h in range(MINE):
            own_same(h).wait_send()
            own_cross(h).wait_send()

    @pl.when(has_behind & has_ahead)
    def _():
        for h in (0, 2, 3):
            relay(h, 0).wait_send()
            relay(h, 1).wait_send()

    @pl.when(has_two)
    def _():
        round_same().wait_send()
        round_cross().wait_send()

    @pl.when(up_two)
    def _():
        round_on(0).wait_send()
        round_on(1).wait_send()

    @pl.when(has_far)
    def _():
        for h in range(LAST):
            far(h, 0).wait_send()
            far(h, 1).wait_send()
        back(0).wait_send()
        back(1).wait_send()

    @pl.when(down_two)
    def _():
        back_on(0).wait_send()
        back_on(1).wait_send()

    @pl.when(has_behind)
    def _():
        for h in range(MINE):
            near(h, 0).wait_send()
            near(h, 1).wait_send()


def body(n, queries, keys, values, d_out):
    dma = pltpu.SemaphoreType.DMA
    wide = (TOK_DEV, HEADS, HEAD_WIDTH)
    slim = (TOK_DEV, KV_HEADS, HEAD_WIDTH)
    return pl.pallas_call(
        functools.partial(kernel, n),
        out_shape=(
            jax.ShapeDtypeStruct(wide, BF16),
            jax.ShapeDtypeStruct(slim, BF16),
            jax.ShapeDtypeStruct(slim, BF16),
        ),
        in_specs=[pl.BlockSpec(memory_space=pltpu.HBM)] * 4,
        out_specs=(pl.BlockSpec(memory_space=pltpu.VMEM),) * 3,
        scratch_shapes=[
            pltpu.VMEM((2,) + slim, BF16),
            pltpu.VMEM((2,) + wide, BF16),
            pltpu.VMEM((2, TOK_DEV * KV_HEADS, HEAD_WIDTH), F32),
            pltpu.VMEM((2, TOK_DEV * HEADS, HEAD_WIDTH), F32),
            pltpu.VMEM((KV_HEADS, 2, TOK_DEV, HEAD_WIDTH), BF16),
            pltpu.VMEM((KV_HEADS, 2, ROWS, HEAD_WIDTH), BF16),
            pltpu.VMEM((TOK_DEV * HEADS, HEAD_WIDTH), F32),
            pltpu.VMEM((2, TOK_DEV * KV_HEADS, HEAD_WIDTH), F32),
            pltpu.VMEM((MINE, 2, SPAN, HEAD_WIDTH), BF16),
            pltpu.VMEM((MINE, 2, 2 * ROWS, HEAD_WIDTH), BF16),
            pltpu.VMEM((MINE, 2, SPAN, HEAD_WIDTH), F32),
            pltpu.VMEM((MINE, 2, 2, TOK_DEV, HEAD_WIDTH), BF16),
            pltpu.VMEM((MINE, 2, 2, TOK_DEV, HEAD_WIDTH), BF16),
            pltpu.VMEM((MINE, 2, 2, TOK_DEV, HEAD_WIDTH), BF16),
            pltpu.VMEM((KV_HEADS, 2, TOK_DEV, HEAD_WIDTH), BF16),
            pltpu.VMEM((MINE, ROWS, HEAD_WIDTH), BF16),
            pltpu.VMEM((MINE, ROWS, HEAD_WIDTH), BF16),
            pltpu.VMEM((MINE, 2, TOK_DEV, HEAD_WIDTH), F32),
            pltpu.VMEM((2, CHIP_TOK, HEAD_WIDTH), BF16),
            pltpu.VMEM((2, 2, TOK_DEV, HEAD_WIDTH), BF16),
            pltpu.VMEM((2, 2, TOK_DEV, HEAD_WIDTH), BF16),
            dma((4,)),
        ]
        + [dma((MINE,))] * 6
        + [dma((MINE, 2))] * 7
        + [dma((KV_HEADS,))]
        + [dma((MINE,))] * 4
        + [dma((2,))] * 7,
        compiler_params=pltpu.CompilerParams(collective_id=0, has_side_effects=True, vmem_limit_bytes=48000 * 1024),
    )(*(pltpu.with_memory_space_constraint(a, pltpu.HBM) for a in (queries, keys, values, d_out)))


def solution(mesh):
    placed = P("ctx", None, None)
    return jax.shard_map(
        functools.partial(body, mesh.shape["ctx"]),
        mesh=mesh,
        in_specs=(placed,) * 4,
        out_specs=(placed,) * 3,
        check_vma=False,
    )
```

```python
import functools

import jax
import jax.numpy as jnp
from jax import lax
from jax.experimental import pallas as pl
from jax.experimental.pallas import tpu as pltpu
from jax.sharding import PartitionSpec as P

HEADS = 16
KV_HEADS = 8
HEAD_WIDTH = 128
WINDOW = 512
TOK_DEV = 128
GROUP = HEADS // KV_HEADS
CHIP_TOK = 2 * TOK_DEV
SPAN = WINDOW + CHIP_TOK
REACH = WINDOW + TOK_DEV
ROWS = GROUP * TOK_DEV
MINE = KV_HEADS // 2
ROUND = 1
LAST = MINE - 1
RING = 4

MESH = pl.DeviceIdType.MESH
SCALE = 168.0 ** (-0.5)
HIDDEN = -1e30
F32 = jnp.float32
BF16 = jnp.bfloat16


def dot(a, b, contract):
    return lax.dot_general(a, b, ((contract[:1], contract[1:]), ((), ())), preferred_element_type=F32)


def kernel(
    n, q_in, k_in, v_in, do_in, dq_out, dk_out, dv_out,
    kraw, qraw, kwide, qwide, kv_in, qd_in, dq_wide, dkv_wide,
    kvb, qdb, acc, p0_out, p0_in, s_out, s_in, dq_send, dq_got, dkv_got, rb, cb, pc_in,
    raw_s, loc_kv, loc_qd, xkv_s, xkv_r, xqd_s, xqd_r, own_s, own_r, fwd_s, fwd_r,
    p0_s, p0_r, sum_s, sum_r, dq_s, dq_r, dkv_s, dkv_r,
    b1_s, b1_r, b2_s, c1_s, c1_r, c2_s, c2_r,
):
    me = lax.axis_index("ctx")
    chip = me // 2
    core = me % 2
    other = 1 - core
    partner = chip * 2 + other
    ahead = (me + 2) % n
    ahead_other = (partner + 2) % n
    behind = (me + n - 2) % n
    behind_other = (partner + n - 2) % n
    last = n // 2 - 1
    has_ahead = chip < last
    has_behind = chip > 0
    has_far = chip > 1
    row = chip // RING * RING
    up = row + (chip + 1) % RING
    down = row + (chip + RING - 1) % RING
    has_two = chip + 2 <= last
    up_two = up + 2 <= last
    down_two = down >= 2

    def ring_of(c, d):
        return c // RING * RING + (c + d) % RING

    def dev(c, k):
        return c * 2 + k

    barrier = pltpu.get_barrier_semaphore()

    def greet(*peers):
        for peer in peers:
            pl.semaphore_signal(barrier, inc=1, device_id=(peer,), device_id_type=MESH)

    greet(partner)
    greet(dev(up, 0), dev(up, 1), dev(down, core))
    pl.when(has_behind)(lambda: greet(behind, behind_other))
    depth = chip // RING % 16
    early = chip < n // 8
    for d in (1, 2):
        pl.when(early & (depth >= d))(lambda d=d: greet(dev(chip - RING * d, core)))
    pl.when(has_far)(lambda: greet(dev(ring_of(chip - 2, RING - 1), core)))
    pl.when(has_two)(lambda: greet(dev(ring_of(chip + 2, 1), 0), dev(ring_of(chip + 2, 1), 1)))

    raws = [
        pltpu.make_async_copy(src, dst, raw_s.at[i])
        for i, (src, dst) in enumerate(
            ((k_in, kraw.at[0]), (v_in, kraw.at[1]), (q_in, qraw.at[0]), (do_in, qraw.at[1]))
        )
    ]
    for copy in raws:
        copy.start()
    for i in (0, 1):
        raws[i].wait()
        kwide[i] = kraw[i].astype(F32).reshape(TOK_DEV * KV_HEADS, HEAD_WIDTH)
    for g in range(KV_HEADS):
        for i in (0, 1):
            kv_in[g, i] = kwide[i, pl.ds(g, TOK_DEV, KV_HEADS), :].astype(BF16)

    known = 2 * has_ahead.astype(jnp.int32) + up_two.astype(jnp.int32) + 2 * down_two.astype(jnp.int32)
    for d in (1, 2):
        known = known + (early & (depth + d < 16)).astype(jnp.int32)
    pl.semaphore_wait(barrier, 4 + known)

    def remote(src, dst, send, recv, target):
        return pltpu.make_async_remote_copy(
            src_ref=src, dst_ref=dst, send_sem=send, recv_sem=recv, device_id=(target,), device_id_type=MESH
        )

    my_tok = pl.ds(pl.multiple_of(core * TOK_DEV, TOK_DEV), TOK_DEV)
    my_key = pl.ds(pl.multiple_of(WINDOW + core * TOK_DEV, TOK_DEV), TOK_DEV)
    my_back = pl.ds(pl.multiple_of(CHIP_TOK + core * TOK_DEV, TOK_DEV), TOK_DEV)
    my_row = pl.ds(pl.multiple_of(core * ROWS, ROWS), ROWS)
    other_tok = pl.ds(pl.multiple_of(WINDOW + other * TOK_DEV, TOK_DEV), TOK_DEV)
    other_row = pl.ds(pl.multiple_of(other * ROWS, ROWS), ROWS)

    def local_kv(h):
        return pltpu.make_async_copy(kv_in.at[core * MINE + h], kvb.at[h, :, my_key, :], loc_kv.at[h])

    def local_qd(h):
        return pltpu.make_async_copy(qd_in.at[core * MINE + h], qdb.at[h, :, my_row, :], loc_qd.at[h])

    def swap_kv(h):
        return remote(kv_in.at[other * MINE + h], kvb.at[h, :, my_key, :], xkv_s.at[h], xkv_r.at[h], partner)

    def swap_qd(h):
        return remote(qd_in.at[other * MINE + h], qdb.at[h, :, my_row, :], xqd_s.at[h], xqd_r.at[h], partner)

    def own_same(h):
        return remote(kv_in.at[core * MINE + h], kvb.at[h, :, my_back, :], own_s.at[h, 0], own_r.at[h, core], ahead)

    def own_cross(h):
        return remote(kv_in.at[other * MINE + h], kvb.at[h, :, my_back, :], own_s.at[h, 1], own_r.at[h, core], ahead_other)

    def came(h, j):
        tok = pl.ds(pl.multiple_of(CHIP_TOK + j * TOK_DEV, TOK_DEV), TOK_DEV)
        return remote(kvb.at[h, :, tok, :], kvb.at[h, :, tok, :], own_s.at[h, j], own_r.at[h, j], ahead)

    def relay(h, j):
        tok = pl.ds(pl.multiple_of(CHIP_TOK + j * TOK_DEV, TOK_DEV), TOK_DEV)
        to = pl.ds(pl.multiple_of(j * TOK_DEV, TOK_DEV), TOK_DEV)
        return remote(kvb.at[h, :, tok, :], kvb.at[h, :, to, :], fwd_s.at[h, j], fwd_r.at[h, j], ahead)

    def far(h, a):
        return remote(p0_out.at[h, a], p0_in.at[h, a], p0_s.at[h, a], p0_r.at[h, a], behind)

    def near(h, a):
        g = core * MINE + h
        return remote(s_out.at[h, a], s_in.at[g], sum_s.at[h, a], sum_r.at[g], behind - core + a)

    def near_in(g):
        return remote(s_in.at[g], s_in.at[g], sum_s.at[0, 0], sum_r.at[g], behind)

    def give_dq(h):
        return remote(dq_send.at[h], dq_got.at[h], dq_s.at[h], dq_r.at[h], partner)

    def give_dkv(h):
        return remote(acc.at[h, :, other_tok, :], dkv_got.at[h], dkv_s.at[h], dkv_r.at[h], partner)

    def round_same():
        return remote(kv_in.at[core * MINE + ROUND], rb.at[:, my_tok, :], b1_s.at[0], b1_r.at[core], dev(down, core))

    def round_cross():
        return remote(kv_in.at[other * MINE + ROUND], rb.at[:, my_tok, :], b1_s.at[1], b1_r.at[core], dev(down, other))

    def round_on(j):
        tok = pl.ds(pl.multiple_of(j * TOK_DEV, TOK_DEV), TOK_DEV)
        return remote(rb.at[:, tok, :], kvb.at[ROUND, :, tok, :], b2_s.at[j], fwd_r.at[ROUND, j], dev(up + 2, core))

    def round_came(j):
        tok = pl.ds(pl.multiple_of(j * TOK_DEV, TOK_DEV), TOK_DEV)
        return remote(rb.at[:, tok, :], rb.at[:, tok, :], b2_s.at[j], b1_r.at[j], ahead)

    def back(a):
        return remote(p0_out.at[LAST, a], cb.at[a], c1_s.at[a], c1_r.at[a], dev(up, core))

    def back_on(a):
        return remote(cb.at[a], pc_in.at[core], c2_s.at[a], c2_r.at[core], dev(down - 2, a))

    def back_came(k):
        return remote(pc_in.at[k], pc_in.at[k], c2_s.at[0], c2_r.at[k], ahead)

    def send_own(h):
        @pl.when(has_ahead)
        def _():
            own_same(h).start()
            own_cross(h).start()

    def pass_on(h, j):
        @pl.when(has_behind)
        def _():
            came(h, j).wait_recv()

        @pl.when(has_behind & has_ahead)
        def _():
            relay(h, j).start()

    def pass_both(h):
        pass_on(h, core)
        pass_on(h, other)

    send_own(0)

    @pl.when(has_two)
    def _():
        round_same().start()
        round_cross().start()

    @pl.when(chip == 1)
    def _():
        for h in range(1, MINE):
            send_own(h)

    for h in range(MINE):
        local_kv(h).start()
        swap_kv(h).start()
    for i in (0, 1):
        raws[2 + i].wait()
        qwide[i] = qraw[i].astype(F32).reshape(TOK_DEV * HEADS, HEAD_WIDTH)
    for g in range(KV_HEADS):
        for i in (0, 1):
            for r in range(GROUP):
                qd_in[g, i, pl.ds(r * TOK_DEV, TOK_DEV), :] = qwide[i, pl.ds(g * GROUP + r, TOK_DEV, HEADS), :].astype(BF16)
    for h in range(MINE):
        local_qd(h).start()
        swap_qd(h).start()

    @pl.when(chip == 0)
    def _():
        kvb[:, :, pl.ds(0, WINDOW), :] = jnp.zeros((MINE, 2, WINDOW, HEAD_WIDTH), BF16)

    @pl.when(chip == 1)
    def _():
        kvb[:, :, pl.ds(0, CHIP_TOK), :] = jnp.zeros((MINE, 2, CHIP_TOK, HEAD_WIDTH), BF16)

    pass_both(0)

    @pl.when(chip != 1)
    def _():
        for h in range(1, MINE):
            send_own(h)

    @pl.when(up_two)
    def _():
        for j in (core, other):
            round_came(j).wait_recv()
            round_on(j).start()

    @pl.when(chip == 2)
    def _():
        pass_both(2)
        pass_both(3)

    first_key = WINDOW - CHIP_TOK * chip

    def keep_dq(g, rows):
        for r in range(GROUP):
            dq_wide[pl.ds(g * GROUP + r, TOK_DEV, HEADS), :] = rows[r * TOK_DEV : (r + 1) * TOK_DEV]

    def half(h, b):
        key_at = pl.ds(b * TOK_DEV, REACH)
        row_at = pl.ds(b * ROWS, ROWS)
        k = kvb[h, 0, key_at, :]
        v = kvb[h, 1, key_at, :]
        q = qdb[h, 0, row_at, :]
        do = qdb[h, 1, row_at, :]
        s = dot(k, q, (1, 1))
        key_at_tile = lax.broadcasted_iota(jnp.int32, (TOK_DEV, ROWS), 0)
        query_at_tile = lax.broadcasted_iota(jnp.int32, (TOK_DEV, ROWS), 1) % TOK_DEV
        later = key_at_tile > query_at_tile
        tiles = [s[i * TOK_DEV : (i + 1) * TOK_DEV] for i in range(REACH // TOK_DEV)]
        tiles[0] = jnp.where(later, tiles[0], HIDDEN)
        tiles[-1] = jnp.where(later, HIDDEN, tiles[-1])
        for i in range(WINDOW // TOK_DEV - b):
            tiles[i] = tiles[i] + jnp.where((b + i) * TOK_DEV >= first_key, 0.0, HIDDEN)
        s = jnp.concatenate(tiles, axis=0)
        top = jnp.max(s, axis=0, keepdims=True)
        e = jnp.exp((s - top) * SCALE)
        p = e * (1.0 / jnp.sum(e, axis=0, keepdims=True))
        low = p.astype(BF16)
        o = dot(v, low, (0, 0)).astype(BF16).astype(F32)
        row_dot = jnp.sum(o * do.astype(F32).T, axis=0, keepdims=True)
        gp = dot(v, do, (1, 1))
        gs = (p * (gp - row_dot)).astype(BF16)
        dv = dot(low, do, (1, 0))
        dk = dot(gs, q, (1, 0)) * SCALE
        dq = (dot(k, gs, (0, 0)) * SCALE).T
        if b == 0:
            acc[h, 0, pl.ds(0, REACH), :] = dk
            acc[h, 1, pl.ds(0, REACH), :] = dv
            acc[h, 0, pl.ds(REACH, TOK_DEV), :] = jnp.zeros((TOK_DEV, HEAD_WIDTH), F32)
            acc[h, 1, pl.ds(REACH, TOK_DEV), :] = jnp.zeros((TOK_DEV, HEAD_WIDTH), F32)
        else:
            acc[h, 0, key_at, :] += dk
            acc[h, 1, key_at, :] += dv

        @pl.when(core == b)
        def _():
            keep_dq(core * MINE + h, dq)

        @pl.when(core != b)
        def _():
            dq_send[h] = dq.astype(BF16)

    def send_far(h, a):
        @pl.when(has_far)
        def _():
            p0_out[h, a] = acc[h, :, pl.ds(a * TOK_DEV, TOK_DEV), :].astype(BF16)

        @pl.when(has_far & (h < LAST))
        def _():
            far(h, a).start()

        @pl.when(has_far & (h == LAST))
        def _():
            back(a).start()

    def add_near(h, a):
        at = pl.ds(CHIP_TOK + a * TOK_DEV, TOK_DEV)

        @pl.when(has_behind & has_ahead & (h < LAST))
        def _():
            far(h, a).wait_recv()
            s_out[h, a] = (acc[h, :, at, :] + p0_in[h, a].astype(F32)).astype(BF16)

        @pl.when((chip == last) | (h == LAST))
        def _():
            s_out[h, a] = acc[h, :, at, :].astype(BF16)

        @pl.when(has_behind)
        def _():
            near(h, a).start()

    def finish(g, own):
        @pl.when(has_ahead)
        def _():
            near_in(g).wait_recv()

        @pl.when(chip == last)
        def _():
            s_in[g] = jnp.zeros((2, TOK_DEV, HEAD_WIDTH), BF16)

        total = own + s_in[g].astype(F32)
        for i in (0, 1):
            dkv_wide[i, pl.ds(g, TOK_DEV, KV_HEADS), :] = total[i]

    def finish_both(h):
        give_dkv(h).wait_recv()
        finish(core * MINE + h, acc[h, :, my_key, :])
        finish(other * MINE + h, dkv_got[h])

    def add_both(h):
        add_near(h, 0)
        add_near(h, 1)

    def step(h, carry):
        local_kv(h).wait()
        local_qd(h).wait()
        swap_kv(h).wait_recv()
        swap_qd(h).wait_recv()

        @pl.when(has_far)
        def _():
            relay(h, 0).wait_recv()
            relay(h, 1).wait_recv()

        @pl.when(has_behind & (h == ROUND))
        def _():
            came(ROUND, 0).wait_recv()
            came(ROUND, 1).wait_recv()

        half(h, 0)
        send_far(h, 0)

        half(h, 1)
        send_far(h, 1)
        give_dq(h).start()
        give_dkv(h).start()

        @pl.when((h == 1) & (chip != 2))
        def _():
            pass_both(2)

        @pl.when(h == 1)
        def _():
            add_both(0)

        @pl.when((h == 1) & (chip != 2))
        def _():
            pass_both(3)

        @pl.when(h == 1)
        def _():
            add_both(1)

        @pl.when(h == 2)
        def _():
            finish_both(0)

        return carry

    lax.fori_loop(0, MINE, step, 0)
    add_both(LAST)
    add_both(2)

    @pl.when(down_two)
    def _():
        for a in (0, 1):
            back(a).wait_recv()
            back_on(a).start()

    finish_both(1)
    for h in range(MINE):
        give_dq(h).wait_recv()
        keep_dq(other * MINE + h, dq_got[h].astype(F32))
    dq_out[...] = dq_wide[...].astype(BF16).reshape(TOK_DEV, HEADS, HEAD_WIDTH)
    finish_both(2)
    give_dkv(LAST).wait_recv()

    @pl.when(has_two)
    def _():
        back_came(0).wait_recv()
        back_came(1).wait_recv()

    @pl.when(chip + 2 > last)
    def _():
        pc_in[...] = jnp.zeros_like(pc_in)

    finish(core * MINE + LAST, acc[LAST, :, my_key, :] + pc_in[core].astype(F32))
    finish(other * MINE + LAST, dkv_got[LAST] + pc_in[other].astype(F32))
    dk_out[...] = dkv_wide[0].astype(BF16).reshape(TOK_DEV, KV_HEADS, HEAD_WIDTH)
    dv_out[...] = dkv_wide[1].astype(BF16).reshape(TOK_DEV, KV_HEADS, HEAD_WIDTH)

    for h in range(MINE):
        swap_kv(h).wait_send()
        swap_qd(h).wait_send()
        give_dq(h).wait_send()
        give_dkv(h).wait_send()

    @pl.when(has_ahead)
    def _():
        for h in range(MINE):
            own_same(h).wait_send()
            own_cross(h).wait_send()

    @pl.when(has_behind & has_ahead)
    def _():
        for h in (0, 2, 3):
            relay(h, 0).wait_send()
            relay(h, 1).wait_send()

    @pl.when(has_two)
    def _():
        round_same().wait_send()
        round_cross().wait_send()

    @pl.when(up_two)
    def _():
        round_on(0).wait_send()
        round_on(1).wait_send()

    @pl.when(has_far)
    def _():
        for h in range(LAST):
            far(h, 0).wait_send()
            far(h, 1).wait_send()
        back(0).wait_send()
        back(1).wait_send()

    @pl.when(down_two)
    def _():
        back_on(0).wait_send()
        back_on(1).wait_send()

    @pl.when(has_behind)
    def _():
        for h in range(MINE):
            near(h, 0).wait_send()
            near(h, 1).wait_send()


def put(*refs):
    copies = [pltpu.make_async_copy(refs[i], refs[3 + i], refs[6].at[i]) for i in range(3)]
    for copy in copies:
        copy.start()
    for copy in copies:
        copy.wait()


def body(n, queries, keys, values, d_out):
    dma = pltpu.SemaphoreType.DMA
    wide = (TOK_DEV, HEADS, HEAD_WIDTH)
    slim = (TOK_DEV, KV_HEADS, HEAD_WIDTH)
    grads = pl.pallas_call(
        functools.partial(kernel, n),
        out_shape=(
            jax.ShapeDtypeStruct(wide, BF16),
            jax.ShapeDtypeStruct(slim, BF16),
            jax.ShapeDtypeStruct(slim, BF16),
        ),
        in_specs=[pl.BlockSpec(memory_space=pltpu.HBM)] * 4,
        out_specs=(pl.BlockSpec(memory_space=pltpu.VMEM),) * 3,
        scratch_shapes=[
            pltpu.VMEM((2,) + slim, BF16),
            pltpu.VMEM((2,) + wide, BF16),
            pltpu.VMEM((2, TOK_DEV * KV_HEADS, HEAD_WIDTH), F32),
            pltpu.VMEM((2, TOK_DEV * HEADS, HEAD_WIDTH), F32),
            pltpu.VMEM((KV_HEADS, 2, TOK_DEV, HEAD_WIDTH), BF16),
            pltpu.VMEM((KV_HEADS, 2, ROWS, HEAD_WIDTH), BF16),
            pltpu.VMEM((TOK_DEV * HEADS, HEAD_WIDTH), F32),
            pltpu.VMEM((2, TOK_DEV * KV_HEADS, HEAD_WIDTH), F32),
            pltpu.VMEM((MINE, 2, SPAN, HEAD_WIDTH), BF16),
            pltpu.VMEM((MINE, 2, 2 * ROWS, HEAD_WIDTH), BF16),
            pltpu.VMEM((MINE, 2, SPAN, HEAD_WIDTH), F32),
            pltpu.VMEM((MINE, 2, 2, TOK_DEV, HEAD_WIDTH), BF16),
            pltpu.VMEM((MINE, 2, 2, TOK_DEV, HEAD_WIDTH), BF16),
            pltpu.VMEM((MINE, 2, 2, TOK_DEV, HEAD_WIDTH), BF16),
            pltpu.VMEM((KV_HEADS, 2, TOK_DEV, HEAD_WIDTH), BF16),
            pltpu.VMEM((MINE, ROWS, HEAD_WIDTH), BF16),
            pltpu.VMEM((MINE, ROWS, HEAD_WIDTH), BF16),
            pltpu.VMEM((MINE, 2, TOK_DEV, HEAD_WIDTH), F32),
            pltpu.VMEM((2, CHIP_TOK, HEAD_WIDTH), BF16),
            pltpu.VMEM((2, 2, TOK_DEV, HEAD_WIDTH), BF16),
            pltpu.VMEM((2, 2, TOK_DEV, HEAD_WIDTH), BF16),
            dma((4,)),
        ]
        + [dma((MINE,))] * 6
        + [dma((MINE, 2))] * 7
        + [dma((KV_HEADS,))]
        + [dma((MINE,))] * 4
        + [dma((2,))] * 7,
        compiler_params=pltpu.CompilerParams(collective_id=0, has_side_effects=True, vmem_limit_bytes=48000 * 1024),
    )(*(pltpu.with_memory_space_constraint(a, pltpu.HBM) for a in (queries, keys, values, d_out)))
    return pl.pallas_call(
        put,
        out_shape=tuple(jax.ShapeDtypeStruct(g.shape, g.dtype) for g in grads),
        in_specs=[pl.BlockSpec(memory_space=pltpu.VMEM)] * 3,
        out_specs=(pl.BlockSpec(memory_space=pltpu.HBM),) * 3,
        scratch_shapes=[dma((3,))],
        compiler_params=pltpu.CompilerParams(vmem_limit_bytes=32 * 2**20),
    )(*grads)


def solution(mesh):
    placed = P("ctx", None, None)
    return jax.shard_map(
        functools.partial(body, mesh.shape["ctx"]),
        mesh=mesh,
        in_specs=(placed,) * 4,
        out_specs=(placed,) * 3,
        check_vma=False,
    )
```

```python
import functools

import jax
import jax.numpy as jnp
from jax import lax
from jax.experimental import pallas as pl
from jax.experimental.pallas import tpu as pltpu
from jax.sharding import PartitionSpec as P

HEADS = 16
KV_HEADS = 8
HEAD_WIDTH = 128
WINDOW = 512
TOK_DEV = 128
GROUP = HEADS // KV_HEADS
CHIP_TOK = 2 * TOK_DEV
SPAN = WINDOW + CHIP_TOK
REACH = WINDOW + TOK_DEV
ROWS = GROUP * TOK_DEV
MINE = KV_HEADS // 2
ROUND = 1
LAST = MINE - 1
RING = 4

MESH = pl.DeviceIdType.MESH
SCALE = 168.0 ** (-0.5)
HIDDEN = -1e30
F32 = jnp.float32
BF16 = jnp.bfloat16


def dot(a, b, contract):
    return lax.dot_general(a, b, ((contract[:1], contract[1:]), ((), ())), preferred_element_type=F32)


def kernel(
    n, q_in, k_in, v_in, do_in, dq_out, dk_out, dv_out,
    kraw, qraw, kwide, qwide, kv_in, qd_in, dq_wide, dkv_wide,
    kvb, qdb, acc, p0_out, p0_in, s_out, s_in, dq_send, dq_got, dkv_got, rb, cb, pc_in,
    raw_s, loc_kv, loc_qd, xkv_s, xkv_r, xqd_s, xqd_r, own_s, own_r, fwd_s, fwd_r,
    p0_s, p0_r, sum_s, sum_r, dq_s, dq_r, dkv_s, dkv_r,
    b1_s, b1_r, b2_s, c1_s, c1_r, c2_s, c2_r,
):
    me = lax.axis_index("ctx")
    chip = me // 2
    core = me % 2
    other = 1 - core
    partner = chip * 2 + other
    ahead = (me + 2) % n
    ahead_other = (partner + 2) % n
    behind = (me + n - 2) % n
    behind_other = (partner + n - 2) % n
    last = n // 2 - 1
    has_ahead = chip < last
    has_behind = chip > 0
    has_far = chip > 1
    row = chip // RING * RING
    up = row + (chip + 1) % RING
    down = row + (chip + RING - 1) % RING
    has_two = chip + 2 <= last
    up_two = up + 2 <= last
    down_two = down >= 2

    def ring_of(c, d):
        return c // RING * RING + (c + d) % RING

    def dev(c, k):
        return c * 2 + k

    barrier = pltpu.get_barrier_semaphore()

    def greet(*peers):
        for peer in peers:
            pl.semaphore_signal(barrier, inc=1, device_id=(peer,), device_id_type=MESH)

    greet(partner)
    greet(dev(up, 0), dev(up, 1), dev(down, core))
    pl.when(has_behind)(lambda: greet(behind, behind_other))
    depth = chip // RING % 16
    early = chip < n // 8
    for d in (2,):
        pl.when(early & (depth >= d))(lambda d=d: greet(dev(chip - RING * d, core)))
    pl.when(has_far)(lambda: greet(dev(ring_of(chip - 2, RING - 1), core)))
    pl.when(has_two)(lambda: greet(dev(ring_of(chip + 2, 1), 0), dev(ring_of(chip + 2, 1), 1)))

    raws = [
        pltpu.make_async_copy(src, dst, raw_s.at[i])
        for i, (src, dst) in enumerate(
            ((k_in, kraw.at[0]), (v_in, kraw.at[1]), (q_in, qraw.at[0]), (do_in, qraw.at[1]))
        )
    ]
    for copy in raws:
        copy.start()
    for i in (0, 1):
        raws[i].wait()
        kwide[i] = kraw[i].astype(F32).reshape(TOK_DEV * KV_HEADS, HEAD_WIDTH)
    for g in range(KV_HEADS):
        for i in (0, 1):
            kv_in[g, i] = kwide[i, pl.ds(g, TOK_DEV, KV_HEADS), :].astype(BF16)

    known = 2 * has_ahead.astype(jnp.int32) + up_two.astype(jnp.int32) + 2 * down_two.astype(jnp.int32)
    for d in (2,):
        known = known + (early & (depth + d < 16)).astype(jnp.int32)
    pl.semaphore_wait(barrier, 4 + known)

    def remote(src, dst, send, recv, target):
        return pltpu.make_async_remote_copy(
            src_ref=src, dst_ref=dst, send_sem=send, recv_sem=recv, device_id=(target,), device_id_type=MESH
        )

    my_tok = pl.ds(pl.multiple_of(core * TOK_DEV, TOK_DEV), TOK_DEV)
    my_key = pl.ds(pl.multiple_of(WINDOW + core * TOK_DEV, TOK_DEV), TOK_DEV)
    my_back = pl.ds(pl.multiple_of(CHIP_TOK + core * TOK_DEV, TOK_DEV), TOK_DEV)
    my_row = pl.ds(pl.multiple_of(core * ROWS, ROWS), ROWS)
    other_tok = pl.ds(pl.multiple_of(WINDOW + other * TOK_DEV, TOK_DEV), TOK_DEV)
    other_row = pl.ds(pl.multiple_of(other * ROWS, ROWS), ROWS)

    def local_kv(h):
        return pltpu.make_async_copy(kv_in.at[core * MINE + h], kvb.at[h, :, my_key, :], loc_kv.at[h])

    def local_qd(h):
        return pltpu.make_async_copy(qd_in.at[core * MINE + h], qdb.at[h, :, my_row, :], loc_qd.at[h])

    def swap_kv(h):
        return remote(kv_in.at[other * MINE + h], kvb.at[h, :, my_key, :], xkv_s.at[h], xkv_r.at[h], partner)

    def swap_qd(h):
        return remote(qd_in.at[other * MINE + h], qdb.at[h, :, my_row, :], xqd_s.at[h], xqd_r.at[h], partner)

    def own_same(h):
        return remote(kv_in.at[core * MINE + h], kvb.at[h, :, my_back, :], own_s.at[h, 0], own_r.at[h, core], ahead)

    def own_cross(h):
        return remote(kv_in.at[other * MINE + h], kvb.at[h, :, my_back, :], own_s.at[h, 1], own_r.at[h, core], ahead_other)

    def came(h, j):
        tok = pl.ds(pl.multiple_of(CHIP_TOK + j * TOK_DEV, TOK_DEV), TOK_DEV)
        return remote(kvb.at[h, :, tok, :], kvb.at[h, :, tok, :], own_s.at[h, j], own_r.at[h, j], ahead)

    def relay(h, j):
        tok = pl.ds(pl.multiple_of(CHIP_TOK + j * TOK_DEV, TOK_DEV), TOK_DEV)
        to = pl.ds(pl.multiple_of(j * TOK_DEV, TOK_DEV), TOK_DEV)
        return remote(kvb.at[h, :, tok, :], kvb.at[h, :, to, :], fwd_s.at[h, j], fwd_r.at[h, j], ahead)

    def far(h, a):
        return remote(p0_out.at[h, a], p0_in.at[h, a], p0_s.at[h, a], p0_r.at[h, a], behind)

    def near(h, a):
        g = core * MINE + h
        return remote(s_out.at[h, a], s_in.at[g], sum_s.at[h, a], sum_r.at[g], behind - core + a)

    def near_in(g):
        return remote(s_in.at[g], s_in.at[g], sum_s.at[0, 0], sum_r.at[g], behind)

    def give_dq(h):
        return remote(dq_send.at[h], dq_got.at[h], dq_s.at[h], dq_r.at[h], partner)

    def give_dkv(h):
        return remote(acc.at[h, :, other_tok, :], dkv_got.at[h], dkv_s.at[h], dkv_r.at[h], partner)

    def round_same():
        return remote(kv_in.at[core * MINE + ROUND], rb.at[:, my_tok, :], b1_s.at[0], b1_r.at[core], dev(down, core))

    def round_cross():
        return remote(kv_in.at[other * MINE + ROUND], rb.at[:, my_tok, :], b1_s.at[1], b1_r.at[core], dev(down, other))

    def round_on(j):
        tok = pl.ds(pl.multiple_of(j * TOK_DEV, TOK_DEV), TOK_DEV)
        return remote(rb.at[:, tok, :], kvb.at[ROUND, :, tok, :], b2_s.at[j], fwd_r.at[ROUND, j], dev(up + 2, core))

    def round_came(j):
        tok = pl.ds(pl.multiple_of(j * TOK_DEV, TOK_DEV), TOK_DEV)
        return remote(rb.at[:, tok, :], rb.at[:, tok, :], b2_s.at[j], b1_r.at[j], ahead)

    def back(a):
        return remote(p0_out.at[LAST, a], cb.at[a], c1_s.at[a], c1_r.at[a], dev(up, core))

    def back_on(a):
        return remote(cb.at[a], pc_in.at[core], c2_s.at[a], c2_r.at[core], dev(down - 2, a))

    def back_came(k):
        return remote(pc_in.at[k], pc_in.at[k], c2_s.at[0], c2_r.at[k], ahead)

    def send_own(h):
        @pl.when(has_ahead)
        def _():
            own_same(h).start()
            own_cross(h).start()

    def pass_on(h, j):
        @pl.when(has_behind)
        def _():
            came(h, j).wait_recv()

        @pl.when(has_behind & has_ahead)
        def _():
            relay(h, j).start()

    def pass_both(h):
        pass_on(h, core)
        pass_on(h, other)

    send_own(0)

    @pl.when(has_two)
    def _():
        round_same().start()
        round_cross().start()

    @pl.when(chip == 1)
    def _():
        for h in range(1, MINE):
            send_own(h)

    for h in range(MINE):
        local_kv(h).start()
        swap_kv(h).start()
    for i in (0, 1):
        raws[2 + i].wait()
        qwide[i] = qraw[i].astype(F32).reshape(TOK_DEV * HEADS, HEAD_WIDTH)
    for g in range(KV_HEADS):
        for i in (0, 1):
            for r in range(GROUP):
                qd_in[g, i, pl.ds(r * TOK_DEV, TOK_DEV), :] = qwide[i, pl.ds(g * GROUP + r, TOK_DEV, HEADS), :].astype(BF16)
    for h in range(MINE):
        local_qd(h).start()
        swap_qd(h).start()

    @pl.when(chip == 0)
    def _():
        kvb[:, :, pl.ds(0, WINDOW), :] = jnp.zeros((MINE, 2, WINDOW, HEAD_WIDTH), BF16)

    @pl.when(chip == 1)
    def _():
        kvb[:, :, pl.ds(0, CHIP_TOK), :] = jnp.zeros((MINE, 2, CHIP_TOK, HEAD_WIDTH), BF16)

    pass_both(0)

    @pl.when(chip != 1)
    def _():
        for h in range(1, MINE):
            send_own(h)

    def round_both():
        for j in (core, other):
            round_came(j).wait_recv()
            round_on(j).start()

    pl.when(up_two & (chip != RING - 1))(round_both)

    @pl.when(chip == 2)
    def _():
        pass_both(2)
        pass_both(3)

    first_key = WINDOW - CHIP_TOK * chip

    def keep_dq(g, rows):
        for r in range(GROUP):
            dq_wide[pl.ds(g * GROUP + r, TOK_DEV, HEADS), :] = rows[r * TOK_DEV : (r + 1) * TOK_DEV]

    def half(h, b):
        key_at = pl.ds(b * TOK_DEV, REACH)
        row_at = pl.ds(b * ROWS, ROWS)
        k = kvb[h, 0, key_at, :]
        v = kvb[h, 1, key_at, :]
        q = qdb[h, 0, row_at, :]
        do = qdb[h, 1, row_at, :]
        s = dot(k, q, (1, 1))
        key_at_tile = lax.broadcasted_iota(jnp.int32, (TOK_DEV, ROWS), 0)
        query_at_tile = lax.broadcasted_iota(jnp.int32, (TOK_DEV, ROWS), 1) % TOK_DEV
        later = key_at_tile > query_at_tile
        tiles = [s[i * TOK_DEV : (i + 1) * TOK_DEV] for i in range(REACH // TOK_DEV)]
        tiles[0] = jnp.where(later, tiles[0], HIDDEN)
        tiles[-1] = jnp.where(later, HIDDEN, tiles[-1])
        for i in range(WINDOW // TOK_DEV - b):
            tiles[i] = tiles[i] + jnp.where((b + i) * TOK_DEV >= first_key, 0.0, HIDDEN)
        s = jnp.concatenate(tiles, axis=0)
        top = jnp.max(s, axis=0, keepdims=True)
        e = jnp.exp((s - top) * SCALE)
        p = e * (1.0 / jnp.sum(e, axis=0, keepdims=True))
        low = p.astype(BF16)
        o = dot(v, low, (0, 0)).astype(BF16).astype(F32)
        row_dot = jnp.sum(o * do.astype(F32).T, axis=0, keepdims=True)
        gp = dot(v, do, (1, 1))
        gs = (p * (gp - row_dot)).astype(BF16)
        dv = dot(low, do, (1, 0))
        dk = dot(gs, q, (1, 0)) * SCALE
        dq = (dot(k, gs, (0, 0)) * SCALE).T
        if b == 0:
            acc[h, 0, pl.ds(0, REACH), :] = dk
            acc[h, 1, pl.ds(0, REACH), :] = dv
            acc[h, 0, pl.ds(REACH, TOK_DEV), :] = jnp.zeros((TOK_DEV, HEAD_WIDTH), F32)
            acc[h, 1, pl.ds(REACH, TOK_DEV), :] = jnp.zeros((TOK_DEV, HEAD_WIDTH), F32)
        else:
            acc[h, 0, key_at, :] += dk
            acc[h, 1, key_at, :] += dv

        @pl.when(core == b)
        def _():
            keep_dq(core * MINE + h, dq)

        @pl.when(core != b)
        def _():
            dq_send[h] = dq.astype(BF16)

    def send_far(h, a):
        @pl.when(has_far)
        def _():
            p0_out[h, a] = acc[h, :, pl.ds(a * TOK_DEV, TOK_DEV), :].astype(BF16)

        @pl.when(has_far & (h < LAST))
        def _():
            far(h, a).start()

        @pl.when(has_far & (h == LAST))
        def _():
            back(a).start()

    def add_near(h, a):
        at = pl.ds(CHIP_TOK + a * TOK_DEV, TOK_DEV)

        @pl.when(has_behind & has_ahead & (h < LAST))
        def _():
            far(h, a).wait_recv()
            s_out[h, a] = (acc[h, :, at, :] + p0_in[h, a].astype(F32)).astype(BF16)

        @pl.when((chip == last) | (h == LAST))
        def _():
            s_out[h, a] = acc[h, :, at, :].astype(BF16)

        @pl.when(has_behind)
        def _():
            near(h, a).start()

    def finish(g, own):
        @pl.when(has_ahead)
        def _():
            near_in(g).wait_recv()

        @pl.when(chip == last)
        def _():
            s_in[g] = jnp.zeros((2, TOK_DEV, HEAD_WIDTH), BF16)

        total = own + s_in[g].astype(F32)
        for i in (0, 1):
            dkv_wide[i, pl.ds(g, TOK_DEV, KV_HEADS), :] = total[i]

    def finish_both(h):
        give_dkv(h).wait_recv()
        finish(core * MINE + h, acc[h, :, my_key, :])
        finish(other * MINE + h, dkv_got[h])

    def add_both(h):
        add_near(h, 0)
        add_near(h, 1)

    def step(h, carry):
        local_kv(h).wait()
        local_qd(h).wait()
        swap_kv(h).wait_recv()
        swap_qd(h).wait_recv()

        @pl.when(has_far)
        def _():
            relay(h, 0).wait_recv()
            relay(h, 1).wait_recv()

        @pl.when(has_behind & (h == ROUND))
        def _():
            came(ROUND, 0).wait_recv()
            came(ROUND, 1).wait_recv()

        half(h, 0)
        send_far(h, 0)

        pl.when(up_two & (chip == RING - 1) & (h == 0))(round_both)
        half(h, 1)
        send_far(h, 1)
        give_dq(h).start()
        give_dkv(h).start()

        @pl.when((h == 1) & (chip != 2))
        def _():
            pass_both(2)

        @pl.when(h == 1)
        def _():
            add_both(0)

        @pl.when((h == 1) & (chip != 2))
        def _():
            pass_both(3)

        @pl.when(h == 1)
        def _():
            add_both(1)

        @pl.when(h == 2)
        def _():
            finish_both(0)

        return carry

    lax.fori_loop(0, MINE, step, 0)
    add_both(LAST)
    add_both(2)

    @pl.when(down_two)
    def _():
        for a in (0, 1):
            back(a).wait_recv()
            back_on(a).start()

    finish_both(1)
    for h in range(MINE):
        give_dq(h).wait_recv()
        keep_dq(other * MINE + h, dq_got[h].astype(F32))
    dq_out[...] = dq_wide[...].astype(BF16).reshape(TOK_DEV, HEADS, HEAD_WIDTH)
    finish_both(2)
    give_dkv(LAST).wait_recv()

    @pl.when(has_two)
    def _():
        back_came(0).wait_recv()
        back_came(1).wait_recv()

    @pl.when(chip + 2 > last)
    def _():
        pc_in[...] = jnp.zeros_like(pc_in)

    finish(core * MINE + LAST, acc[LAST, :, my_key, :] + pc_in[core].astype(F32))
    finish(other * MINE + LAST, dkv_got[LAST] + pc_in[other].astype(F32))
    dk_out[...] = dkv_wide[0].astype(BF16).reshape(TOK_DEV, KV_HEADS, HEAD_WIDTH)
    dv_out[...] = dkv_wide[1].astype(BF16).reshape(TOK_DEV, KV_HEADS, HEAD_WIDTH)

    for h in range(MINE):
        swap_kv(h).wait_send()
        swap_qd(h).wait_send()
        give_dq(h).wait_send()
        give_dkv(h).wait_send()

    @pl.when(has_ahead)
    def _():
        for h in range(MINE):
            own_same(h).wait_send()
            own_cross(h).wait_send()

    @pl.when(has_behind & has_ahead)
    def _():
        for h in (0, 2, 3):
            relay(h, 0).wait_send()
            relay(h, 1).wait_send()

    @pl.when(has_two)
    def _():
        round_same().wait_send()
        round_cross().wait_send()

    @pl.when(up_two)
    def _():
        round_on(0).wait_send()
        round_on(1).wait_send()

    @pl.when(has_far)
    def _():
        for h in range(LAST):
            far(h, 0).wait_send()
            far(h, 1).wait_send()
        back(0).wait_send()
        back(1).wait_send()

    @pl.when(down_two)
    def _():
        back_on(0).wait_send()
        back_on(1).wait_send()

    @pl.when(has_behind)
    def _():
        for h in range(MINE):
            near(h, 0).wait_send()
            near(h, 1).wait_send()


def put(*refs):
    copies = [pltpu.make_async_copy(refs[i], refs[3 + i], refs[6].at[i]) for i in range(3)]
    for copy in copies:
        copy.start()
    for copy in copies:
        copy.wait()


def body(n, queries, keys, values, d_out):
    dma = pltpu.SemaphoreType.DMA
    wide = (TOK_DEV, HEADS, HEAD_WIDTH)
    slim = (TOK_DEV, KV_HEADS, HEAD_WIDTH)
    grads = pl.pallas_call(
        functools.partial(kernel, n),
        out_shape=(
            jax.ShapeDtypeStruct(wide, BF16),
            jax.ShapeDtypeStruct(slim, BF16),
            jax.ShapeDtypeStruct(slim, BF16),
        ),
        in_specs=[pl.BlockSpec(memory_space=pltpu.HBM)] * 4,
        out_specs=(pl.BlockSpec(memory_space=pltpu.VMEM),) * 3,
        scratch_shapes=[
            pltpu.VMEM((2,) + slim, BF16),
            pltpu.VMEM((2,) + wide, BF16),
            pltpu.VMEM((2, TOK_DEV * KV_HEADS, HEAD_WIDTH), F32),
            pltpu.VMEM((2, TOK_DEV * HEADS, HEAD_WIDTH), F32),
            pltpu.VMEM((KV_HEADS, 2, TOK_DEV, HEAD_WIDTH), BF16),
            pltpu.VMEM((KV_HEADS, 2, ROWS, HEAD_WIDTH), BF16),
            pltpu.VMEM((TOK_DEV * HEADS, HEAD_WIDTH), F32),
            pltpu.VMEM((2, TOK_DEV * KV_HEADS, HEAD_WIDTH), F32),
            pltpu.VMEM((MINE, 2, SPAN, HEAD_WIDTH), BF16),
            pltpu.VMEM((MINE, 2, 2 * ROWS, HEAD_WIDTH), BF16),
            pltpu.VMEM((MINE, 2, SPAN, HEAD_WIDTH), F32),
            pltpu.VMEM((MINE, 2, 2, TOK_DEV, HEAD_WIDTH), BF16),
            pltpu.VMEM((MINE, 2, 2, TOK_DEV, HEAD_WIDTH), BF16),
            pltpu.VMEM((MINE, 2, 2, TOK_DEV, HEAD_WIDTH), BF16),
            pltpu.VMEM((KV_HEADS, 2, TOK_DEV, HEAD_WIDTH), BF16),
            pltpu.VMEM((MINE, ROWS, HEAD_WIDTH), BF16),
            pltpu.VMEM((MINE, ROWS, HEAD_WIDTH), BF16),
            pltpu.VMEM((MINE, 2, TOK_DEV, HEAD_WIDTH), F32),
            pltpu.VMEM((2, CHIP_TOK, HEAD_WIDTH), BF16),
            pltpu.VMEM((2, 2, TOK_DEV, HEAD_WIDTH), BF16),
            pltpu.VMEM((2, 2, TOK_DEV, HEAD_WIDTH), BF16),
            dma((4,)),
        ]
        + [dma((MINE,))] * 6
        + [dma((MINE, 2))] * 7
        + [dma((KV_HEADS,))]
        + [dma((MINE,))] * 4
        + [dma((2,))] * 7,
        compiler_params=pltpu.CompilerParams(collective_id=0, has_side_effects=True, vmem_limit_bytes=48000 * 1024),
    )(*(pltpu.with_memory_space_constraint(a, pltpu.HBM) for a in (queries, keys, values, d_out)))
    return pl.pallas_call(
        put,
        out_shape=tuple(jax.ShapeDtypeStruct(g.shape, g.dtype) for g in grads),
        in_specs=[pl.BlockSpec(memory_space=pltpu.VMEM)] * 3,
        out_specs=(pl.BlockSpec(memory_space=pltpu.HBM),) * 3,
        scratch_shapes=[dma((3,))],
        compiler_params=pltpu.CompilerParams(vmem_limit_bytes=32 * 2**20),
    )(*grads)


def solution(mesh):
    placed = P("ctx", None, None)
    return jax.shard_map(
        functools.partial(body, mesh.shape["ctx"]),
        mesh=mesh,
        in_specs=(placed,) * 4,
        out_specs=(placed,) * 3,
        check_vma=False,
    )
```
